32 devices in a mesh: dp: 4 (over x, core), seq: 8 (over z, y).
Axes of the slice: x: 2, y: 2, z: 4, core: 2. Of those that a mesh axis runs over, the one named last changes fastest.
Arguments:
- queries: bfloat16 [4, 1536, 2048], P('dp', 'seq'), may hold values from -24 to 24
- key_rows: bfloat16 [4, 1536, 2048], P('dp', 'seq'), may hold values from -24 to 24
- value_rows: bfloat16 [4, 1536, 2048], P('dp', 'seq'), may hold values from -6 to 6
- out_weight: bfloat16 [2048, 3072], P('seq'), may hold values from -3 to 3
- cotangent: bfloat16 [4, 1536, 3072], P('dp', 'seq'), may hold values from -0.119628906 to 0.119628906
- tile_lists: int32 [16, 24, 16], replicated, may hold values from 0 to 23, as said below
- live_counts: int32 [16, 24], replicated, may hold values from 1 to 16, as said below
Outputs:
- block_out: bfloat16 [4, 1536, 3072], P('dp', 'seq')
- grad_queries: bfloat16 [4, 1536, 2048], P('dp', 'seq')
- grad_keys: bfloat16 [4, 1536, 2048], P('dp', 'seq')
- grad_values: bfloat16 [4, 1536, 2048], P('dp', 'seq')
- grad_weight: float32 [2048, 3072], P('seq')
The draws below stay inside these ranges and needn't reach their ends.
Inputs may be any that keep to these rules, and one draw needn't show every extreme that they name: `tile_lists`: the 16 entries of a list are distinct tile numbers, and the first is the query tile itself. `live_counts`: every head has a query tile whose 16 entries are all live.
All inputs are finite; a program needn't handle non-finite values.
Results may differ from the reference program's by a relative error of at most 0.015.
Values may be sent and summed in bfloat16 or wider, within the bound.
No kernel may reach another device: no remote copies, remote signals or barrier semaphores. Data moves between devices by JAX's collectives and lax.ppermute only.
A program may use at most 256 MiB of HBM per device.

```python
import jax
import jax.numpy as jnp
from jax import lax

D = 3072
HEADS = 16
HDIM = 128
TILE = 64
KSEL = 16
TOK_DEV = 192
HD = 2048
SEQ_LEN = 1536
CLIPS = 4
N_SEQ = 8


def drawn_pair(key):
    base_key = jax.random.fold_in(key, 17)
    subkeys = jax.random.split(base_key, 2)
    full_shape = (CLIPS, SEQ_LEN, HD)
    query_draw = jnp.clip(jax.random.normal(subkeys[0], full_shape, jnp.float32), -4.0, 4.0)
    key_draw = jnp.clip(jax.random.normal(subkeys[1], full_shape, jnp.float32), -4.0, 4.0)
    return (query_draw, key_draw)


def draw_queries(key, part):
    return drawn_pair(key)[0].astype(jnp.bfloat16)


def draw_key_rows(key, part):
    return drawn_pair(key)[1].astype(jnp.bfloat16)


def draw_tile_lists(key, part):
    block_count = SEQ_LEN // TILE
    random_rank = jax.random.randint(jax.random.fold_in(key, 5), (HEADS, block_count, block_count), 0, 2 ** 20)
    column_index = lax.broadcasted_iota(jnp.int32, (HEADS, block_count, block_count), 2)
    row_index = lax.broadcasted_iota(jnp.int32, (HEADS, block_count, block_count), 1)
    ordering = random_rank * block_count + column_index
    ordering = jnp.where(row_index == column_index, -1, ordering)
    selection = jnp.argsort(ordering, axis=-1)[:, :, :KSEL]
    return selection.astype(jnp.int32)


def draw_live_counts(key, part):
    block_count = SEQ_LEN // TILE
    subkeys = jax.random.split(jax.random.fold_in(key, 7), 3)
    head_cap = jax.random.randint(subkeys[0], (HEADS, 1), (KSEL + 1) // 2, KSEL + 1)
    drawn = jax.random.randint(subkeys[1], (HEADS, block_count), 1, head_cap + 1)
    full_block = jax.random.randint(subkeys[2], (HEADS, 1), 0, block_count)
    block_index = lax.broadcasted_iota(jnp.int32, (HEADS, block_count), 1)
    return jnp.where(block_index == full_block, KSEL, drawn).astype(jnp.int32)


def shard_levels(stream_key, dims, cuts, least, top_value):
    def one(axis_at, parts):
        draws = jax.random.uniform(jax.random.fold_in(jax.random.fold_in(stream_key, 6), axis_at), (parts,), jnp.float32, least / len(cuts), top_value / len(cuts))
        return jnp.repeat(jnp.exp(draws), dims[axis_at] // parts).reshape((-1,) + (1,) * (len(dims) - axis_at - 1))

    loudness = one(*cuts[0])
    for cut in cuts[1:]:
        loudness = loudness * one(*cut)
    return loudness


def noise(own_key, shape, spread, bound, pieces=(), held_as=jnp.bfloat16):
    values = spread * jax.random.normal(own_key, shape, jnp.float32)
    if pieces:
        values = values * shard_levels(own_key, shape, pieces, -0.22, 0.18)
    return jnp.clip(values, -bound, bound).astype(held_as)


def setup_inputs(seed: int = 0) -> dict:
    seeds = jax.random.split(jax.random.key(seed), 8)
    queries = draw_queries(jax.random.fold_in(seeds[7], 71), 0)
    key_rows = draw_key_rows(jax.random.fold_in(seeds[7], 71), 0)
    value_rows = noise(seeds[2], (CLIPS, SEQ_LEN, HD), 1.0, 6.0, ((0, 4), (1, 8)))
    out_weight = noise(seeds[3], (HD, D), 0.5, 3.0, ((0, 8),))
    cotangent = noise(seeds[4], (CLIPS, SEQ_LEN, D), 0.02, 0.119628906, ((0, 4), (1, 8)))
    tile_lists = draw_tile_lists(jax.random.fold_in(seeds[7], 71), 0)
    live_counts = draw_live_counts(jax.random.fold_in(seeds[7], 71), 0)
    return {"queries": queries, "key_rows": key_rows, "value_rows": value_rows, "out_weight": out_weight, "cotangent": cotangent, "tile_lists": tile_lists, "live_counts": live_counts}


def tile_weights(query_tiles, key_tiles, tile_list, live_count, score_scale):
    scores = jnp.einsum("bie,bsje->bisj", query_tiles.astype(jnp.float32), key_tiles.astype(jnp.float32), precision=lax.Precision.HIGHEST) * score_scale
    slot_index = lax.broadcasted_iota(jnp.int32, tile_list.shape, 1)
    live_mask = (slot_index < live_count[:, None])[:, None, :, None]
    masked = jnp.where(live_mask, scores, -jnp.inf)
    row_max = jnp.max(masked, axis=(2, 3), keepdims=True)
    weights = jnp.where(live_mask, jnp.exp(scores - row_max), jnp.float32(0.0))
    return weights / jnp.sum(weights, axis=(2, 3), keepdims=True)


def select_tiles(matrix, tile_list):
    block_count = matrix.shape[0] // TILE
    return matrix.reshape(block_count, TILE, matrix.shape[1])[tile_list]


def head_forward(head_query, head_keys, head_values, tile_list, live_count):
    feature_width = head_query.shape[1]
    score_scale = feature_width ** -0.5
    query_tiles = head_query.reshape(-1, TILE, feature_width)
    weights = tile_weights(query_tiles, select_tiles(head_keys, tile_list), tile_list, live_count, score_scale)
    rounded = weights.astype(jnp.bfloat16)
    result = jnp.einsum("bisj,bsje->bie", rounded.astype(jnp.float32), select_tiles(head_values, tile_list).astype(jnp.float32), precision=lax.Precision.HIGHEST)
    return result.astype(jnp.bfloat16).reshape(head_query.shape)


def head_backward(head_query, head_keys, head_values, head_grad, tile_list, live_count):
    feature_width = head_query.shape[1]
    score_scale = feature_width ** -0.5
    block_count = head_query.shape[0] // TILE
    query_tiles = head_query.reshape(block_count, TILE, feature_width)
    grad_tiles = head_grad.reshape(block_count, TILE, feature_width)
    key_tiles = select_tiles(head_keys, tile_list)
    value_tiles = select_tiles(head_values, tile_list)
    weights = tile_weights(query_tiles, key_tiles, tile_list, live_count, score_scale)
    rounded = weights.astype(jnp.bfloat16)
    grad_probs = jnp.einsum("bie,bsje->bisj", grad_tiles.astype(jnp.float32), value_tiles.astype(jnp.float32), precision=lax.Precision.HIGHEST)
    row_dot = jnp.sum(weights * grad_probs, axis=(2, 3), keepdims=True)
    grad_scores = (weights * (grad_probs - row_dot)).astype(jnp.bfloat16)
    grad_query = jnp.einsum("bisj,bsje->bie", grad_scores.astype(jnp.float32), key_tiles.astype(jnp.float32), precision=lax.Precision.HIGHEST) * score_scale
    key_terms = jnp.einsum("bisj,bie->bsje", grad_scores.astype(jnp.float32), query_tiles.astype(jnp.float32), precision=lax.Precision.HIGHEST) * score_scale
    value_terms = jnp.einsum("bisj,bie->bsje", rounded.astype(jnp.float32), grad_tiles.astype(jnp.float32), precision=lax.Precision.HIGHEST)
    flat_tiles = tile_list.reshape(-1)
    grad_key = jnp.zeros((block_count, TILE, feature_width), jnp.float32).at[flat_tiles].add(key_terms.reshape(-1, TILE, feature_width))
    grad_value = jnp.zeros((block_count, TILE, feature_width), jnp.float32).at[flat_tiles].add(value_terms.reshape(-1, TILE, feature_width))
    return (grad_query.astype(jnp.bfloat16).reshape(head_query.shape),
            grad_key.astype(jnp.bfloat16).reshape(head_query.shape),
            grad_value.astype(jnp.bfloat16).reshape(head_query.shape))


def split_heads(matrix):
    return matrix.reshape(SEQ_LEN, HEADS, HDIM).transpose(1, 0, 2)


def join_heads(stacked):
    return stacked.transpose(1, 0, 2).reshape(SEQ_LEN, HD)


def reference(queries, key_rows, value_rows, out_weight, cotangent, tile_lists, live_counts):
    group_cols = HD // N_SEQ

    def one_clip(weight_acc, operands):
        clip_query, clip_keys, clip_values, clip_grad = operands
        head_items = (split_heads(clip_query), split_heads(clip_keys), split_heads(clip_values), tile_lists, live_counts)
        attn = join_heads(lax.map(lambda item: head_forward(*item), head_items))
        attn_groups = attn.reshape(SEQ_LEN, N_SEQ, group_cols).transpose(1, 0, 2)
        weight_groups = out_weight.reshape(N_SEQ, group_cols, D)

        def add_group(running, pair):
            partial_value = jnp.dot(pair[0], pair[1], preferred_element_type=jnp.float32).astype(jnp.bfloat16)
            partial_value = lax.optimization_barrier(partial_value)
            return running + partial_value.astype(jnp.float32), None

        mixed_rows, unused = lax.scan(add_group, jnp.zeros((SEQ_LEN, D), jnp.float32), (attn_groups, weight_groups))
        grad_attn = jnp.dot(clip_grad, out_weight.T, preferred_element_type=jnp.float32).astype(jnp.bfloat16)
        back_items = (split_heads(clip_query), split_heads(clip_keys), split_heads(clip_values), split_heads(grad_attn), tile_lists, live_counts)
        grad_q, grad_k, grad_v = lax.map(lambda item: head_backward(*item), back_items)
        attn_blocks = attn.reshape(N_SEQ, TOK_DEV, HD)
        grad_blocks = clip_grad.reshape(N_SEQ, TOK_DEV, D)

        def add_block(running, pair):
            partial_value = jnp.dot(pair[0].T, pair[1], preferred_element_type=jnp.float32).astype(jnp.bfloat16)
            partial_value = lax.optimization_barrier(partial_value)
            return running + partial_value.astype(jnp.float32), None

        weight_acc, unused = lax.scan(add_block, weight_acc, (attn_blocks, grad_blocks))
        outputs = (mixed_rows.astype(jnp.bfloat16), join_heads(grad_q), join_heads(grad_k), join_heads(grad_v))
        return weight_acc, outputs

    weight_total, stacked = lax.scan(one_clip, jnp.zeros((HD, D), jnp.float32), (queries, key_rows, value_rows, cotangent))
    return (stacked[0], stacked[1], stacked[2], stacked[3], weight_total)
```

```python
import jax
import jax.numpy as jnp
from jax import lax
from jax.experimental import pallas as pl
from jax.experimental.pallas import tpu as pltpu
from jax.sharding import PartitionSpec as P

HDIM = 128
TILE = 64
SCALE = HDIM**-0.5
EXP2_SCALE = SCALE * 1.4426950408889634
NEG = -1e30
VMEM_LIMIT = 48 * 1024 * 1024
BF16 = jnp.bfloat16
F32 = jnp.float32


def params(**kw):
    return pltpu.CompilerParams(vmem_limit_bytes=VMEM_LIMIT, **kw)


def dot_nt(a, b):
    return lax.dot_general(a, b, (((1,), (1,)), ((), ())), preferred_element_type=F32)


def dot_nn(a, b):
    return lax.dot_general(a, b, (((1,), (0,)), ((), ())), preferred_element_type=F32)


def pack_heads(arrays, n):
    rows, width = arrays[0].shape
    cols = width // n
    count = len(arrays)

    def body(*refs):
        out, sem = refs[count], refs[count + 1]
        copies = [
            pltpu.make_async_copy(
                refs[a].at[:, pl.ds(j * cols, cols)], out.at[j, a], sem.at[j * count + a]
            )
            for j in range(n)
            for a in range(count)
        ]
        for copy in copies:
            copy.start()
        for copy in copies:
            copy.wait()

    return pl.pallas_call(
        body,
        out_shape=jax.ShapeDtypeStruct((n, count, rows, cols), arrays[0].dtype),
        in_specs=[pl.BlockSpec(memory_space=pl.ANY)] * count,
        out_specs=pl.BlockSpec(memory_space=pl.ANY),
        scratch_shapes=[pltpu.SemaphoreType.DMA((n * count,))],
        name="pack_heads",
    )(*arrays)


def unpack_heads(packed):
    n, count, rows, cols = packed.shape

    def body(*refs):
        src, outs, sem = refs[0], refs[1 : 1 + count], refs[1 + count]
        copies = [
            pltpu.make_async_copy(
                src.at[j, a], outs[a].at[:, pl.ds(j * cols, cols)], sem.at[j * count + a]
            )
            for j in range(n)
            for a in range(count)
        ]
        for copy in copies:
            copy.start()
        for copy in copies:
            copy.wait()

    return pl.pallas_call(
        body,
        out_shape=[jax.ShapeDtypeStruct((rows, n * cols), packed.dtype)] * count,
        in_specs=[pl.BlockSpec(memory_space=pl.ANY)],
        out_specs=[pl.BlockSpec(memory_space=pl.ANY)] * count,
        scratch_shapes=[pltpu.SemaphoreType.DMA((n * count,))],
        name="unpack_heads",
    )(packed)


def masked_scores(q, k, bias):
    s = dot_nt(q, k)
    tiles = bias.shape[0]
    s = s.reshape(tiles, TILE, s.shape[1]) + bias[:, None, :]
    return s.reshape(tiles * TILE, s.shape[2])


def masked_probs(q, k, bias):
    s = masked_scores(q, k, bias)
    e = jnp.exp2((s - jnp.max(s, axis=1, keepdims=True)) * EXP2_SCALE)
    return e * (1.0 / jnp.sum(e, axis=1, keepdims=True))


def attention_forward(packed, bias, half):
    n, _, rows, cols = packed.shape
    heads = cols // HDIM
    tokens = n * rows
    q_rows = 2 * rows
    steps = n // 2
    half_steps = steps // 2
    tiles = q_rows // TILE

    def body(half_ref, q_ref, k_ref, v_ref, bias_ref, o_ref):
        q = q_ref[...].reshape(q_rows, HDIM)
        k = k_ref[...].reshape(tokens, HDIM)
        v = v_ref[...].reshape(tokens, HDIM)
        probs = masked_probs(q, k, bias_ref[0, 0]).astype(BF16)
        o_ref[0] = dot_nn(probs, v).astype(BF16)

    return pl.pallas_call(
        body,
        out_shape=jax.ShapeDtypeStruct((2, tokens // 2, cols), BF16),
        grid_spec=pltpu.PrefetchScalarGridSpec(
            num_scalar_prefetch=1,
            grid=(heads, steps),
            in_specs=[
                pl.BlockSpec((2, 1, rows, HDIM), lambda h, i, r: (i, 0, 0, h)),
                pl.BlockSpec((n, 1, rows, HDIM), lambda h, i, r: (0, 1, 0, h)),
                pl.BlockSpec((n, 1, rows, HDIM), lambda h, i, r: (0, 2, 0, h)),
                pl.BlockSpec((1, 1, tiles, tokens), lambda h, i, r: (h, i, 0, 0)),
            ],
            out_specs=pl.BlockSpec(
                (1, q_rows, HDIM), lambda h, i, r: ((i // half_steps) ^ r[0], i % half_steps, h)
            ),
        ),
        compiler_params=params(),
        name="attention_forward",
    )(half, packed, packed, packed, bias)


def attention_backward(packed, bias, half, grad_own, grad_mirror):
    n, _, rows, cols = packed.shape
    heads = cols // HDIM
    tokens = n * rows
    q_rows = 2 * rows
    steps = n // 2
    half_steps = steps // 2
    tiles = q_rows // TILE

    def body(half_ref, q_ref, k_ref, v_ref, bias_ref, g0_ref, g1_ref, out_ref, dk_ref, dv_ref):
        i = pl.program_id(1)
        q = q_ref[...].reshape(q_rows, HDIM)
        k = k_ref[...].reshape(tokens, HDIM)
        v = v_ref[...].reshape(tokens, HDIM)
        own = (i // half_steps) == half_ref[0]
        grad = jnp.where(own, g0_ref[...], g1_ref[...])
        probs = masked_probs(q, k, bias_ref[0, 0])
        grad_probs = dot_nt(grad, v)
        row_dot = jnp.sum(probs * grad_probs, axis=1, keepdims=True)
        grad_scores = (probs * (grad_probs - row_dot)).astype(BF16)
        grad_q = dot_nn(grad_scores, k) * SCALE
        out_ref[pl.ds(2 * i, 2), 0] = grad_q.astype(BF16).reshape(2, rows, HDIM)
        dk_t = dot_nn(q.T, grad_scores)
        dv_t = dot_nn(grad.T, probs.astype(BF16))

        @pl.when(i == 0)
        def _():
            dk_ref[...] = dk_t
            dv_ref[...] = dv_t

        @pl.when(i > 0)
        def _():
            dk_ref[...] += dk_t
            dv_ref[...] += dv_t

        @pl.when(i == steps - 1)
        def _():
            out_ref[:, 1] = (dk_ref[...] * SCALE).T.astype(BF16).reshape(n, rows, HDIM)
            out_ref[:, 2] = dv_ref[...].T.astype(BF16).reshape(n, rows, HDIM)

    return pl.pallas_call(
        body,
        out_shape=jax.ShapeDtypeStruct((n, 3, rows, cols), BF16),
        grid_spec=pltpu.PrefetchScalarGridSpec(
            num_scalar_prefetch=1,
            grid=(heads, steps),
            in_specs=[
                pl.BlockSpec((2, 1, rows, HDIM), lambda h, i, r: (i, 0, 0, h)),
                pl.BlockSpec((n, 1, rows, HDIM), lambda h, i, r: (0, 1, 0, h)),
                pl.BlockSpec((n, 1, rows, HDIM), lambda h, i, r: (0, 2, 0, h)),
                pl.BlockSpec((1, 1, tiles, tokens), lambda h, i, r: (h, i, 0, 0)),
                pl.BlockSpec((q_rows, HDIM), lambda h, i, r: (i % half_steps, h)),
                pl.BlockSpec((q_rows, HDIM), lambda h, i, r: (i % half_steps, h)),
            ],
            out_specs=pl.BlockSpec((n, 3, rows, HDIM), lambda h, i, r: (0, 0, 0, h)),
            scratch_shapes=[pltpu.VMEM((HDIM, tokens), F32), pltpu.VMEM((HDIM, tokens), F32)],
        ),
        compiler_params=params(),
        name="attention_backward",
    )(half, packed, packed, packed, bias, grad_own, grad_mirror)


def attention_grad(cot_blocks, w_own, w_mirror, rank):
    m = len(cot_blocks)
    rows, width = cot_blocks[0].shape
    cols = w_own.shape[0]

    def body(rank_ref, *refs):
        cots, w0_ref, w1_ref, g0_ref, g1_ref = refs[:m], *refs[m:]
        for j in range(m):
            start = pl.multiple_of((rank_ref[0] ^ j) * rows, rows)
            g0_ref[pl.ds(start, rows), :] = dot_nt(cots[j][...], w0_ref[...]).astype(BF16)
            g1_ref[pl.ds(start, rows), :] = dot_nt(cots[j][...], w1_ref[...]).astype(BF16)

    full = lambda shape: pl.BlockSpec(shape, lambda i, r: (0, 0))
    return pl.pallas_call(
        body,
        out_shape=[jax.ShapeDtypeStruct((m * rows, cols), BF16)] * 2,
        grid_spec=pltpu.PrefetchScalarGridSpec(
            num_scalar_prefetch=1,
            grid=(1,),
            in_specs=[full((rows, width))] * m + [full((cols, width))] * 2,
            out_specs=[full((m * rows, cols))] * 2,
        ),
        compiler_params=params(),
        name="attention_grad",
    )(rank, *cot_blocks, w_own, w_mirror)


def output_partial(attn_own, attn_mirror, w_own, w_mirror, m):
    tokens, cols = attn_own.shape
    width = w_own.shape[1]
    rows = tokens // m
    step = 512

    def body(a0_ref, a1_ref, w0_ref, w1_ref, o_ref):
        total = dot_nn(a0_ref[...], w0_ref[...]) + dot_nn(a1_ref[...], w1_ref[...])
        o_ref[...] = total.astype(BF16).reshape(m, rows, step)

    return pl.pallas_call(
        body,
        out_shape=jax.ShapeDtypeStruct((m, rows, width), BF16),
        grid=(width // step,),
        in_specs=[
            pl.BlockSpec((tokens, cols), lambda i: (0, 0)),
            pl.BlockSpec((tokens, cols), lambda i: (0, 0)),
            pl.BlockSpec((cols, step), lambda i: (0, i)),
            pl.BlockSpec((cols, step), lambda i: (0, i)),
        ],
        out_specs=pl.BlockSpec((m, rows, step), lambda i: (0, 0, i)),
        compiler_params=params(),
        name="output_partial",
    )(attn_own, attn_mirror, w_own, w_mirror)


def weight_grad_partial(attn_own, attn_mirror, cot_blocks, rank, parts):
    m = len(cot_blocks)
    rows, width = cot_blocks[0].shape
    tokens, cols = attn_own.shape
    step = 512
    piece = cols // parts

    def body(rank_ref, *refs):
        a0_ref, a1_ref, cots, o_ref, at_ref = refs[0], refs[1], refs[2 : 2 + m], *refs[2 + m :]

        @pl.when(pl.program_id(0) == 0)
        def _():
            for j in range(m):
                start = pl.multiple_of((rank_ref[0] ^ j) * rows, rows)
                at_ref[j, :cols] = a0_ref[pl.ds(start, rows), :].T
                at_ref[j, cols:] = a1_ref[pl.ds(start, rows), :].T

        total = dot_nn(at_ref[0], cots[0][...])
        for j in range(1, m):
            total += dot_nn(at_ref[j], cots[j][...])
        total = total.astype(BF16).reshape(2, parts, piece, step)
        o_ref[:, 0] = total[0]
        o_ref[:, 1] = total[1]

    return pl.pallas_call(
        body,
        out_shape=jax.ShapeDtypeStruct((parts, 2, piece, width), BF16),
        grid_spec=pltpu.PrefetchScalarGridSpec(
            num_scalar_prefetch=1,
            grid=(width // step,),
            in_specs=[pl.BlockSpec((tokens, cols), lambda i, r: (0, 0))] * 2
            + [pl.BlockSpec((rows, step), lambda i, r: (0, i))] * m,
            out_specs=pl.BlockSpec((parts, 2, piece, step), lambda i, r: (0, 0, 0, i)),
            scratch_shapes=[pltpu.VMEM((m, 2 * cols, rows), BF16)],
        ),
        compiler_params=params(),
        name="weight_grad_partial",
    )(rank, attn_own, attn_mirror, *cot_blocks)


def mask_bias(my_tiles, my_counts, tokens, q_rows):
    heads, blocks, slots = my_tiles.shape
    key_tile = lax.broadcasted_iota(jnp.int32, (1, 1, tokens, 1), 2) // TILE
    slot = lax.broadcasted_iota(jnp.int32, (1, 1, 1, slots), 3)
    seen = (my_tiles[:, :, None, :] == key_tile) & (slot < my_counts[:, :, None, None])
    bias = jnp.where(jnp.any(seen, axis=3), F32(0.0), F32(NEG))
    tiles = q_rows // TILE
    return bias.reshape(heads, blocks // tiles, tiles, tokens)


def shards(queries, key_rows, value_rows, out_weight, cotangent, tile_lists, live_counts):
    n = lax.axis_size("seq")
    dp = lax.axis_size("dp")
    m = n // 2
    s = lax.axis_index("seq")
    d = lax.axis_index("dp")
    half = (s // m).astype(jnp.int32).reshape(1)
    rank = (s % m).astype(jnp.int32).reshape(1)
    rows = queries.shape[1]
    cols, width = out_weight.shape
    heads = cols // HDIM
    xor = lambda x, bit: lax.ppermute(x, "seq", [(i, i ^ bit) for i in range(n)])

    my_tiles = lax.dynamic_slice_in_dim(tile_lists, s * heads, heads, 0)
    my_counts = lax.dynamic_slice_in_dim(live_counts, s * heads, heads, 0)
    bias = mask_bias(my_tiles, my_counts, n * rows, 2 * rows)

    packed = pack_heads([queries[0], key_rows[0], value_rows[0]], n)
    packed = lax.all_to_all(packed, "seq", split_axis=0, concat_axis=0, tiled=True)

    piece = cols // dp
    w_piece = lax.dynamic_slice_in_dim(out_weight, d * piece, piece, 0)
    w_mirror = lax.all_gather(xor(w_piece, m), "dp", axis=0, tiled=True)

    cot_at = {0: cotangent[0]}
    bit = m // 2
    while bit:
        cot_at.update({j | bit: xor(block, bit) for j, block in list(cot_at.items())})
        bit //= 2
    cot_blocks = [cot_at[j] for j in range(m)]

    grad_own, grad_send = attention_grad(cot_blocks, out_weight, w_mirror, rank)
    grad_mirror = xor(grad_send, m)

    attn = attention_forward(packed, bias, half)
    attn_own = attn[0]
    attn_mirror = xor(attn[1], m)

    grads = attention_backward(packed, bias, half, grad_own, grad_mirror)
    grads = lax.all_to_all(grads, "seq", split_axis=0, concat_axis=0, tiled=True)
    back_q, back_k, back_v = unpack_heads(grads)

    partial = output_partial(attn_own, attn_mirror, out_weight, w_mirror, m)
    groups = [list(range(m)), list(range(m, n))]
    partial = lax.all_to_all(
        partial, "seq", split_axis=0, concat_axis=0, tiled=True, axis_index_groups=groups
    )
    block_out = jnp.sum(partial.astype(F32), axis=0).astype(BF16)

    gw = weight_grad_partial(attn_own, attn_mirror, cot_blocks, rank, dp)
    gw = lax.all_to_all(gw, "dp", split_axis=0, concat_axis=0, tiled=True)
    gw = jnp.sum(gw.astype(F32), axis=0)
    gw = (gw[0] + xor(gw[1].astype(BF16), m).astype(F32)).astype(BF16)
    grad_weight = lax.all_gather(gw, "dp", axis=0, tiled=True).astype(F32)
    return (block_out[None], back_q[None], back_k[None], back_v[None], grad_weight)


def solution(mesh):
    token_spec = P("dp", "seq", None)
    in_specs = (
        token_spec,
        token_spec,
        token_spec,
        P("seq", None),
        token_spec,
        P(),
        P(),
    )
    out_specs = (token_spec,) * 4 + (P("seq", None),)
    return jax.shard_map(shards, mesh=mesh, in_specs=in_specs, out_specs=out_specs, check_vma=False)
```

```python
import jax
import jax.numpy as jnp
from jax import lax
from jax.experimental import pallas as pl
from jax.experimental.pallas import tpu as pltpu
from jax.sharding import PartitionSpec as P

HDIM = 128
TILE = 64
SCALE = HDIM**-0.5
EXP2_SCALE = SCALE * 1.4426950408889634
NEG = -1e30
VMEM_LIMIT = 48 * 1024 * 1024
BF16 = jnp.bfloat16
F32 = jnp.float32


def params(**kw):
    return pltpu.CompilerParams(vmem_limit_bytes=VMEM_LIMIT, **kw)


def cost(flops, nbytes, exps=0):
    return pl.CostEstimate(flops=flops, bytes_accessed=nbytes, transcendentals=exps)


def dot_nt(a, b):
    return lax.dot_general(a, b, (((1,), (1,)), ((), ())), preferred_element_type=F32)


def dot_nn(a, b):
    return lax.dot_general(a, b, (((1,), (0,)), ((), ())), preferred_element_type=F32)


def pack_heads(arrays, n):
    rows, width = arrays[0].shape
    cols = width // n
    count = len(arrays)

    def body(*refs):
        for a in range(count):
            refs[count][0, a] = refs[a][...]

    return pl.pallas_call(
        body,
        out_shape=jax.ShapeDtypeStruct((n, count, rows, cols), arrays[0].dtype),
        grid=(n,),
        in_specs=[pl.BlockSpec((rows, cols), lambda j: (0, j))] * count,
        out_specs=pl.BlockSpec((1, count, rows, cols), lambda j: (j, 0, 0, 0)),
        compiler_params=params(),
        cost_estimate=cost(0, 4 * n * count * rows * cols),
        name="pack_heads",
    )(*arrays)


def unpack_heads(packed):
    heads = len(packed)
    n, count, rows, width = packed[0].shape
    cols = heads * width

    def body(*refs):
        for a in range(count):
            for h in range(heads):
                refs[heads + a][:, h * width : (h + 1) * width] = refs[h][0, a]

    return pl.pallas_call(
        body,
        out_shape=[jax.ShapeDtypeStruct((rows, n * cols), BF16)] * count,
        grid=(n,),
        in_specs=[pl.BlockSpec((1, count, rows, width), lambda j: (j, 0, 0, 0))] * heads,
        out_specs=[pl.BlockSpec((rows, cols), lambda j: (0, j))] * count,
        compiler_params=params(),
        cost_estimate=cost(0, 4 * n * count * rows * cols),
        name="unpack_heads",
    )(*packed)


def masked_scores(q, k, bias):
    s = dot_nt(q, k)
    tiles = bias.shape[0]
    s = s.reshape(tiles, TILE, s.shape[1]) + bias[:, None, :]
    return s.reshape(tiles * TILE, s.shape[2])


def masked_probs(q, k, bias):
    s = masked_scores(q, k, bias)
    e = jnp.exp2((s - jnp.max(s, axis=1, keepdims=True)) * EXP2_SCALE)
    return e * (1.0 / jnp.sum(e, axis=1, keepdims=True))


def attention_forward(packed, bias, half):
    n, _, rows, cols = packed.shape
    heads = cols // HDIM
    tokens = n * rows
    q_rows = 2 * rows
    steps = n // 2
    half_steps = steps // 2
    tiles = q_rows // TILE

    def body(half_ref, q_ref, k_ref, v_ref, bias_ref, own_ref, send_ref):
        q = q_ref[...].reshape(q_rows, HDIM)
        k = k_ref[...].reshape(tokens, HDIM)
        v = v_ref[...].reshape(tokens, HDIM)
        probs = masked_probs(q, k, bias_ref[0, 0]).astype(BF16)
        attn = dot_nn(probs, v).astype(BF16)
        own = (pl.program_id(1) // half_steps) == half_ref[0]

        @pl.when(own)
        def _():
            own_ref[...] = attn

        @pl.when(jnp.logical_not(own))
        def _():
            send_ref[...] = attn

    return pl.pallas_call(
        body,
        out_shape=[jax.ShapeDtypeStruct((tokens // 2, cols), BF16)] * 2,
        grid_spec=pltpu.PrefetchScalarGridSpec(
            num_scalar_prefetch=1,
            grid=(heads, steps),
            in_specs=[
                pl.BlockSpec((2, 1, rows, HDIM), lambda h, i, r: (i, 0, 0, h)),
                pl.BlockSpec((n, 1, rows, HDIM), lambda h, i, r: (0, 1, 0, h)),
                pl.BlockSpec((n, 1, rows, HDIM), lambda h, i, r: (0, 2, 0, h)),
                pl.BlockSpec((1, 1, tiles, tokens), lambda h, i, r: (h, i, 0, 0)),
            ],
            out_specs=[
                pl.BlockSpec(
                    (q_rows, HDIM),
                    lambda h, i, r: (jnp.clip(i - r[0] * half_steps, 0, half_steps - 1), h),
                ),
                pl.BlockSpec(
                    (q_rows, HDIM),
                    lambda h, i, r: (jnp.clip(i - (1 - r[0]) * half_steps, 0, half_steps - 1), h),
                ),
            ],
        ),
        compiler_params=params(),
        cost_estimate=cost(4 * tokens**2 * cols, 8 * tokens * cols, heads * tokens**2),
        name="attention_forward",
    )(half, packed, packed, packed, bias)


def attention_backward(packed, bias, half, grad_own, grad_mirror, head):
    n, _, rows, cols = packed.shape
    tokens = n * rows
    q_rows = 2 * rows
    steps = n // 2
    half_steps = steps // 2
    tiles = q_rows // TILE

    def body(half_ref, q_ref, k_ref, v_ref, bias_ref, g0_ref, g1_ref, out_ref, dk_ref, dv_ref):
        i = pl.program_id(0)
        q = q_ref[...].reshape(q_rows, HDIM)
        k = k_ref[...].reshape(tokens, HDIM)
        v = v_ref[...].reshape(tokens, HDIM)
        own = (i // half_steps) == half_ref[0]
        grad = jnp.where(own, g0_ref[...], g1_ref[...])
        probs = masked_probs(q, k, bias_ref[0, 0])
        grad_probs = dot_nt(grad, v)
        row_dot = jnp.sum(probs * grad_probs, axis=1, keepdims=True)
        grad_scores = (probs * (grad_probs - row_dot)).astype(BF16)
        grad_q = dot_nn(grad_scores, k) * SCALE
        out_ref[pl.ds(2 * i, 2), 0] = grad_q.astype(BF16).reshape(2, rows, HDIM)
        dk_t = dot_nn(q.T, grad_scores)
        dv_t = dot_nn(grad.T, probs.astype(BF16))

        @pl.when(i == 0)
        def _():
            dk_ref[...] = dk_t
            dv_ref[...] = dv_t

        @pl.when(i > 0)
        def _():
            dk_ref[...] += dk_t
            dv_ref[...] += dv_t

        @pl.when(i == steps - 1)
        def _():
            out_ref[:, 1] = (dk_ref[...] * SCALE).T.astype(BF16).reshape(n, rows, HDIM)
            out_ref[:, 2] = dv_ref[...].T.astype(BF16).reshape(n, rows, HDIM)

    return pl.pallas_call(
        body,
        out_shape=jax.ShapeDtypeStruct((n, 3, rows, HDIM), BF16),
        grid_spec=pltpu.PrefetchScalarGridSpec(
            num_scalar_prefetch=1,
            grid=(steps,),
            in_specs=[
                pl.BlockSpec((2, 1, rows, HDIM), lambda i, r: (i, 0, 0, head)),
                pl.BlockSpec((n, 1, rows, HDIM), lambda i, r: (0, 1, 0, head)),
                pl.BlockSpec((n, 1, rows, HDIM), lambda i, r: (0, 2, 0, head)),
                pl.BlockSpec((1, 1, tiles, tokens), lambda i, r: (head, i, 0, 0)),
                pl.BlockSpec((q_rows, HDIM), lambda i, r: (i % half_steps, head)),
                pl.BlockSpec((q_rows, HDIM), lambda i, r: (i % half_steps, head)),
            ],
            out_specs=pl.BlockSpec((n, 3, rows, HDIM), lambda i, r: (0, 0, 0, 0)),
            scratch_shapes=[pltpu.VMEM((HDIM, tokens), F32), pltpu.VMEM((HDIM, tokens), F32)],
        ),
        compiler_params=params(),
        cost_estimate=cost(10 * tokens**2 * HDIM, 14 * tokens * HDIM, tokens**2),
        name="attention_backward",
    )(half, packed, packed, packed, bias, grad_own, grad_mirror)


def attention_grad(cot_blocks, w_own, w_mirror, rank):
    m = len(cot_blocks)
    rows, width = cot_blocks[0].shape
    cols = w_own.shape[0]

    def body(rank_ref, *refs):
        cots, w0_ref, w1_ref, g0_ref, g1_ref = refs[:m], *refs[m:]
        for w_ref, g_ref in ((w1_ref, g1_ref), (w0_ref, g0_ref)):
            for j in range(m):
                start = pl.multiple_of((rank_ref[0] ^ j) * rows, rows)
                g_ref[pl.ds(start, rows), :] = dot_nt(cots[j][...], w_ref[...]).astype(BF16)

    full = lambda shape: pl.BlockSpec(shape, lambda i, r: (0, 0))
    return pl.pallas_call(
        body,
        out_shape=[jax.ShapeDtypeStruct((m * rows, cols), BF16)] * 2,
        grid_spec=pltpu.PrefetchScalarGridSpec(
            num_scalar_prefetch=1,
            grid=(1,),
            in_specs=[full((rows, width))] * m + [full((cols, width))] * 2,
            out_specs=[full((m * rows, cols))] * 2,
        ),
        compiler_params=params(),
        cost_estimate=cost(4 * m * rows * width * cols, 2 * width * (m * rows + 2 * cols)),
        name="attention_grad",
    )(rank, *cot_blocks, w_own, w_mirror)


def output_partial(attn_own, attn_mirror, w_own, w_mirror, rank, m):
    tokens, cols = attn_own.shape
    width = w_own.shape[1]
    rows = tokens // m
    step = 512

    def body(rank_ref, a0_ref, a1_ref, w0_ref, w1_ref, *o_refs):
        for j in range(m):
            at = pl.ds(pl.multiple_of((rank_ref[0] ^ j) * rows, rows), rows)
            total = dot_nn(a0_ref[at, :], w0_ref[...]) + dot_nn(a1_ref[at, :], w1_ref[...])
            o_refs[j][...] = total.astype(BF16)

    return pl.pallas_call(
        body,
        out_shape=[jax.ShapeDtypeStruct((rows, width), BF16)] * m,
        grid_spec=pltpu.PrefetchScalarGridSpec(
            num_scalar_prefetch=1,
            grid=(width // step,),
            in_specs=[pl.BlockSpec((tokens, cols), lambda i, r: (0, 0))] * 2
            + [pl.BlockSpec((cols, step), lambda i, r: (0, i))] * 2,
            out_specs=[pl.BlockSpec((rows, step), lambda i, r: (0, i))] * m,
        ),
        compiler_params=params(),
        cost_estimate=cost(4 * tokens * cols * width, 2 * (2 * cols + tokens) * width),
        name="output_partial",
    )(rank, attn_own, attn_mirror, w_own, w_mirror)


def weight_grad_partial(attn_own, attn_mirror, cot_blocks, rank, place, parts):
    m = len(cot_blocks)
    rows, width = cot_blocks[0].shape
    tokens, cols = attn_own.shape
    step = 512
    piece = cols // parts

    def body(rank_ref, place_ref, *refs):
        a0_ref, a1_ref, cots = refs[0], refs[1], refs[2 : 2 + m]
        keep_ref, send_ref, at_ref, sum_ref = refs[2 + m :]

        @pl.when(pl.program_id(0) == 0)
        def _():
            for j in range(m):
                start = pl.multiple_of((rank_ref[0] ^ j) * rows, rows)
                at_ref[j, :cols] = a0_ref[pl.ds(start, rows), :].T
                at_ref[j, cols:] = a1_ref[pl.ds(start, rows), :].T

        total = dot_nn(at_ref[0], cots[0][...])
        for j in range(1, m):
            total += dot_nn(at_ref[j], cots[j][...])
        sum_ref[...] = total.astype(BF16).reshape(2 * parts, piece, step)
        for j in range(parts):
            out_ref = send_ref if j % 2 else keep_ref
            out_ref[j // 2, 0] = sum_ref[place_ref[0] ^ j]
            out_ref[j // 2, 1] = sum_ref[parts + (place_ref[0] ^ j)]

    shape = (parts // 2, 2, piece, width)
    return pl.pallas_call(
        body,
        out_shape=[jax.ShapeDtypeStruct(shape, BF16)] * 2,
        grid_spec=pltpu.PrefetchScalarGridSpec(
            num_scalar_prefetch=2,
            grid=(width // step,),
            in_specs=[pl.BlockSpec((tokens, cols), lambda i, r, p: (0, 0))] * 2
            + [pl.BlockSpec((rows, step), lambda i, r, p: (0, i))] * m,
            out_specs=[pl.BlockSpec(shape[:3] + (step,), lambda i, r, p: (0, 0, 0, i))] * 2,
            scratch_shapes=[
                pltpu.VMEM((m, 2 * cols, rows), BF16),
                pltpu.VMEM((2 * parts, piece, step), BF16),
            ],
        ),
        compiler_params=params(),
        cost_estimate=cost(4 * tokens * cols * width, 2 * (2 * cols + tokens) * width),
        name="weight_grad_partial",
    )(rank, place, attn_own, attn_mirror, *cot_blocks)


def join_parts(pieces, place, dtype):
    parts = len(pieces)
    rows, width = pieces[0].shape
    step = 1024

    def body(place_ref, *refs):
        for j in range(parts):
            refs[parts][place_ref[0] ^ j] = refs[j][...].astype(dtype)

    joined = pl.pallas_call(
        body,
        out_shape=jax.ShapeDtypeStruct((parts, rows, width), dtype),
        grid_spec=pltpu.PrefetchScalarGridSpec(
            num_scalar_prefetch=1,
            grid=(width // step,),
            in_specs=[pl.BlockSpec((rows, step), lambda i, p: (0, i))] * parts,
            out_specs=pl.BlockSpec((parts, rows, step), lambda i, p: (0, 0, i)),
        ),
        compiler_params=params(),
        cost_estimate=cost(0, 6 * parts * rows * width),
        name="join_parts",
    )(place, *pieces)
    return joined.reshape(parts * rows, width)


def mask_bias(my_tiles, my_counts, tokens, q_rows):
    heads, blocks, slots = my_tiles.shape
    key_tile = lax.broadcasted_iota(jnp.int32, (1, 1, tokens, 1), 2) // TILE
    slot = lax.broadcasted_iota(jnp.int32, (1, 1, 1, slots), 3)
    seen = (my_tiles[:, :, None, :] == key_tile) & (slot < my_counts[:, :, None, None])
    bias = jnp.where(jnp.any(seen, axis=3), F32(0.0), F32(NEG))
    tiles = q_rows // TILE
    return bias.reshape(heads, blocks // tiles, tiles, tokens)


def shards(queries, key_rows, value_rows, out_weight, cotangent, tile_lists, live_counts):
    n = lax.axis_size("seq")
    dp = lax.axis_size("dp")
    m = n // 2
    s = lax.axis_index("seq")
    d = lax.axis_index("dp")
    half = (s // m).astype(jnp.int32).reshape(1)
    rank = (s % m).astype(jnp.int32).reshape(1)
    rows = queries.shape[1]
    cols, width = out_weight.shape
    heads = cols // HDIM
    place = d.astype(jnp.int32).reshape(1)
    xor = lambda x, bit: lax.ppermute(x, "seq", [(i, i ^ bit) for i in range(n)])

    def gather_parts(x):
        pieces = {0: x}
        bit = dp // 2
        while bit:
            pieces.update({j | bit: dp_xor(x, bit) for j, x in list(pieces.items())})
            bit //= 2
        return [pieces[j] for j in range(dp)]

    dp_xor = lambda x, bit: lax.ppermute(x, "dp", [(i, i ^ bit) for i in range(dp)])

    my_tiles = lax.dynamic_slice_in_dim(tile_lists, s * heads, heads, 0)
    my_counts = lax.dynamic_slice_in_dim(live_counts, s * heads, heads, 0)
    bias = mask_bias(my_tiles, my_counts, n * rows, 2 * rows)

    packed = pack_heads([queries[0], key_rows[0], value_rows[0]], n)
    packed = lax.all_to_all(packed, "seq", split_axis=0, concat_axis=0, tiled=True)

    attn_own, attn_send = attention_forward(packed, bias, half)

    piece = cols // dp
    w_piece = xor(lax.dynamic_slice_in_dim(out_weight, d * piece, piece, 0), m)
    bit = m // 2
    cot_at = {0: cotangent[0], bit: xor(cotangent[0], bit)}
    if bit > 1:
        cot_at[1] = xor(cotangent[0], 1)
    attn_send, w_piece, cot_at[bit] = lax.optimization_barrier(
        (attn_send, w_piece, cot_at[bit])
    )
    attn_mirror = xor(attn_send, m)
    w_pieces = gather_parts(w_piece)

    while bit > 1:
        bit //= 2
        for j in list(cot_at):
            if j | bit not in cot_at:
                cot_at[j | bit] = xor(cot_at[j], bit)
    cot_blocks = [cot_at[j] for j in range(m)]

    w_mirror = join_parts(w_pieces, place, BF16)
    grad_own, grad_send = attention_grad(cot_blocks, out_weight, w_mirror, rank)
    grad_mirror = xor(grad_send, m)
    attn_mirror, grad_send = lax.optimization_barrier((attn_mirror, grad_send))
    partials = output_partial(attn_own, attn_mirror, out_weight, w_mirror, rank, m)
    keep, send = weight_grad_partial(attn_own, attn_mirror, cot_blocks, rank, place, dp)
    grad_mirror, partials, keep, send = lax.optimization_barrier(
        (grad_mirror, partials, keep, send)
    )
    sums = [partials[0]] + [xor(partials[j], j) for j in range(1, m)]

    gw = keep.astype(F32) + dp_xor(send, 1).astype(F32)
    bit = 2
    while bit < dp:
        gw = gw[0::2].astype(F32) + dp_xor(gw[1::2].astype(BF16), bit).astype(F32)
        bit *= 2
    gw_own, gw_send = gw[0, 0], gw[0, 1].astype(BF16)

    grads = []
    for head in range(heads):
        if head == 1:
            gw_send, grad_own = lax.optimization_barrier((gw_send, grad_own))
        got = attention_backward(packed, bias, half, grad_own, grad_mirror, head)
        if head == 0:
            got, sums[1:3] = lax.optimization_barrier((got, sums[1:3]))
        else:
            got, sums[3:] = lax.optimization_barrier((got, sums[3:]))
        grads.append(got)
    gw = (gw_own + xor(gw_send, m).astype(F32)).astype(BF16)
    grads = [lax.all_to_all(x, "seq", split_axis=0, concat_axis=0, tiled=True) for x in grads]
    back_q, back_k, back_v = unpack_heads(grads)

    block_out = sum(x.astype(F32) for x in sums).astype(BF16)
    pieces = gather_parts(gw)
    grad_weight = join_parts(pieces, place, F32)
    return (block_out[None], back_q[None], back_k[None], back_v[None], grad_weight)


def solution(mesh):
    token_spec = P("dp", "seq", None)
    in_specs = (
        token_spec,
        token_spec,
        token_spec,
        P("seq", None),
        token_spec,
        P(),
        P(),
    )
    out_specs = (token_spec,) * 4 + (P("seq", None),)
    return jax.shard_map(shards, mesh=mesh, in_specs=in_specs, out_specs=out_specs, check_vma=False)
```

```python
import jax
import jax.numpy as jnp
from jax import lax
from jax.experimental import pallas as pl
from jax.experimental.pallas import tpu as pltpu
from jax.sharding import PartitionSpec as P

HDIM = 128
TILE = 64
SCALE = HDIM**-0.5
EXP2_SCALE = SCALE * 1.4426950408889634
NEG = -1e30
EXTRA = HDIM - 3
VMEM_LIMIT = 48 * 1024 * 1024
BF16 = jnp.bfloat16
F32 = jnp.float32


def params(**kw):
    return pltpu.CompilerParams(vmem_limit_bytes=VMEM_LIMIT, **kw)


def cost(flops, nbytes, exps=0):
    return pl.CostEstimate(flops=flops, bytes_accessed=nbytes, transcendentals=exps)


def dot_nt(a, b):
    return lax.dot_general(a, b, (((1,), (1,)), ((), ())), preferred_element_type=F32)


def dot_nn(a, b):
    return lax.dot_general(a, b, (((1,), (0,)), ((), ())), preferred_element_type=F32)


def pack_heads(arrays, n):
    rows, width = arrays[0].shape
    cols = width // n
    count = len(arrays)

    def body(*refs):
        for a in range(count):
            refs[count][0, a] = refs[a][...]

    return pl.pallas_call(
        body,
        out_shape=jax.ShapeDtypeStruct((n, count, rows, cols), arrays[0].dtype),
        grid=(n,),
        in_specs=[pl.BlockSpec((rows, cols), lambda j: (0, j))] * count,
        out_specs=pl.BlockSpec((1, count, rows, cols), lambda j: (j, 0, 0, 0)),
        compiler_params=params(),
        cost_estimate=cost(0, 4 * n * count * rows * cols),
        name="pack_heads",
    )(*arrays)


def unpack_heads(packed):
    heads = len(packed)
    n, count, rows, width = packed[0].shape
    cols = heads * width

    def body(*refs):
        for a in range(count):
            for h in range(heads):
                refs[heads + a][:, h * width : (h + 1) * width] = refs[h][0, a]

    return pl.pallas_call(
        body,
        out_shape=[jax.ShapeDtypeStruct((rows, n * cols), BF16)] * count,
        grid=(n,),
        in_specs=[pl.BlockSpec((1, count, rows, width), lambda j: (j, 0, 0, 0))] * heads,
        out_specs=[pl.BlockSpec((rows, cols), lambda j: (0, j))] * count,
        compiler_params=params(),
        cost_estimate=cost(0, 4 * n * count * rows * cols),
        name="unpack_heads",
    )(*packed)


def split3(x):
    high = x.astype(BF16)
    rest = x - high.astype(F32)
    mid = rest.astype(BF16)
    low = (rest - mid.astype(F32)).astype(BF16)
    return high, mid, low


def put_columns(base, columns):
    lane = lax.broadcasted_iota(jnp.int32, base.shape, 1)
    for at, column in enumerate(columns):
        base = jnp.where(lane == EXTRA + at, column.astype(F32), base)
    return base


def attention_forward(packed, mask, half):
    n, _, rows, cols = packed.shape
    heads = cols // HDIM
    tokens = n * rows
    q_rows = 2 * rows
    steps = n // 2
    half_steps = steps // 2
    tiles = q_rows // TILE

    def body(half_ref, q_ref, k_ref, v_ref, mask_ref, own_ref, send_ref, extra_ref, wide_ref):
        i = pl.program_id(1)

        @pl.when(i == 0)
        def _():
            wide_ref[:, :HDIM] = k_ref[...].reshape(tokens, HDIM)
            wide_ref[:, HDIM:] = mask_ref[0]

        shape = (q_rows, HDIM)
        tile = lax.broadcasted_iota(jnp.int32, shape, 0) // TILE + i * tiles
        ones = jnp.where(tile == lax.broadcasted_iota(jnp.int32, shape, 1), F32(1), F32(0))
        q = jnp.concatenate([q_ref[...].reshape(shape), ones.astype(BF16)], axis=1)
        s = dot_nt(q, wide_ref[...])
        top = jnp.max(s, axis=1, keepdims=True)
        e = jnp.exp2((s - top) * EXP2_SCALE)
        total = jnp.sum(e, axis=1, keepdims=True)
        attn = dot_nn(e.astype(BF16), v_ref[...].reshape(tokens, HDIM)) * (1.0 / total)
        attn = attn.astype(BF16)
        log_sum = top + jnp.log2(total) * (1.0 / EXP2_SCALE)
        extra_ref[...] = put_columns(ones, split3(log_sum)).astype(BF16)
        own = (i // half_steps) == half_ref[0]

        @pl.when(own)
        def _():
            own_ref[...] = attn

        @pl.when(jnp.logical_not(own))
        def _():
            send_ref[...] = attn

    return pl.pallas_call(
        body,
        out_shape=[jax.ShapeDtypeStruct((tokens // 2, cols), BF16)] * 2
        + [jax.ShapeDtypeStruct((tokens, cols), BF16)],
        grid_spec=pltpu.PrefetchScalarGridSpec(
            num_scalar_prefetch=1,
            grid=(heads, steps),
            in_specs=[
                pl.BlockSpec((2, 1, rows, HDIM), lambda h, i, r: (i, 0, 0, h)),
                pl.BlockSpec((n, 1, rows, HDIM), lambda h, i, r: (0, 1, 0, h)),
                pl.BlockSpec((n, 1, rows, HDIM), lambda h, i, r: (0, 2, 0, h)),
                pl.BlockSpec((1, tokens, HDIM), lambda h, i, r: (h, 0, 0)),
            ],
            out_specs=[
                pl.BlockSpec(
                    (q_rows, HDIM),
                    lambda h, i, r: (jnp.clip(i - r[0] * half_steps, 0, half_steps - 1), h),
                ),
                pl.BlockSpec(
                    (q_rows, HDIM),
                    lambda h, i, r: (jnp.clip(i - (1 - r[0]) * half_steps, 0, half_steps - 1), h),
                ),
                pl.BlockSpec((q_rows, HDIM), lambda h, i, r: (i, h)),
            ],
            scratch_shapes=[pltpu.VMEM((tokens, 2 * HDIM), BF16)],
        ),
        compiler_params=params(),
        cost_estimate=cost(4 * tokens**2 * cols, 8 * tokens * cols, heads * tokens**2),
        name="attention_forward",
    )(half, packed, packed, packed, mask)


def attention_backward(packed, mask, half, extra, attn_own, attn_send, grad_own, grad_mirror, head):
    n, _, rows, cols = packed.shape
    tokens = n * rows
    q_rows = 2 * rows
    steps = n // 2
    half_steps = steps // 2

    def body(half_ref, q_ref, k_ref, v_ref, mask_ref, extra_ref, *refs):
        a0_ref, a1_ref, g0_ref, g1_ref, out_ref, dk_ref, dv_ref, wide_ref, wide_v_ref = refs
        i = pl.program_id(0)

        @pl.when(i == 0)
        def _():
            wide_ref[:, :HDIM] = k_ref[...].reshape(tokens, HDIM)
            wide_ref[:, HDIM:] = mask_ref[0]
            wide_v_ref[:, :HDIM] = v_ref[...].reshape(tokens, HDIM)
            lane = lax.broadcasted_iota(jnp.int32, (tokens, HDIM), 1)
            wide_v_ref[:, HDIM:] = jnp.where(lane >= EXTRA, F32(-1), F32(0)).astype(BF16)

        q = q_ref[...].reshape(q_rows, HDIM)
        own = (i // half_steps) == half_ref[0]
        grad = jnp.where(own, g0_ref[...], g1_ref[...])
        attn = jnp.where(own, a0_ref[...], a1_ref[...])
        row_dot = jnp.sum(grad.astype(F32) * attn.astype(F32), axis=1, keepdims=True)
        zeros = jnp.zeros((q_rows, HDIM), F32)
        wide_grad = jnp.concatenate(
            [grad, put_columns(zeros, split3(row_dot)).astype(BF16)], axis=1
        )
        wide_q = jnp.concatenate([q, extra_ref[...]], axis=1)
        probs = jnp.exp2(dot_nt(wide_q, wide_ref[...]) * EXP2_SCALE)
        grad_scores = (probs * dot_nt(wide_grad, wide_v_ref[...])).astype(BF16)
        grad_q = dot_nn(grad_scores, wide_ref[:, :HDIM]) * SCALE
        out_ref[pl.ds(2 * i, 2), 0] = grad_q.astype(BF16).reshape(2, rows, HDIM)
        dk_t = dot_nn(q.T, grad_scores)
        dv_t = dot_nn(grad.T, probs.astype(BF16))

        @pl.when(i == 0)
        def _():
            dk_ref[...] = dk_t
            dv_ref[...] = dv_t

        @pl.when(i > 0)
        def _():
            dk_ref[...] += dk_t
            dv_ref[...] += dv_t

        @pl.when(i == steps - 1)
        def _():
            out_ref[:, 1] = (dk_ref[...] * SCALE).T.astype(BF16).reshape(n, rows, HDIM)
            out_ref[:, 2] = dv_ref[...].T.astype(BF16).reshape(n, rows, HDIM)

    return pl.pallas_call(
        body,
        out_shape=jax.ShapeDtypeStruct((n, 3, rows, HDIM), BF16),
        grid_spec=pltpu.PrefetchScalarGridSpec(
            num_scalar_prefetch=1,
            grid=(steps,),
            in_specs=[
                pl.BlockSpec((2, 1, rows, HDIM), lambda i, r: (i, 0, 0, head)),
                pl.BlockSpec((n, 1, rows, HDIM), lambda i, r: (0, 1, 0, head)),
                pl.BlockSpec((n, 1, rows, HDIM), lambda i, r: (0, 2, 0, head)),
                pl.BlockSpec((1, tokens, HDIM), lambda i, r: (head, 0, 0)),
                pl.BlockSpec((q_rows, HDIM), lambda i, r: (i, head)),
            ]
            + [pl.BlockSpec((q_rows, HDIM), lambda i, r: (i % half_steps, head))] * 4,
            out_specs=pl.BlockSpec((n, 3, rows, HDIM), lambda i, r: (0, 0, 0, 0)),
            scratch_shapes=[pltpu.VMEM((HDIM, tokens), F32)] * 2
            + [pltpu.VMEM((tokens, 2 * HDIM), BF16)] * 2,
        ),
        compiler_params=params(),
        cost_estimate=cost(10 * tokens**2 * HDIM, 14 * tokens * HDIM, tokens**2),
        name="attention_backward",
    )(half, packed, packed, packed, mask, extra, attn_own, attn_send, grad_own, grad_mirror)


def attention_grad(cot_blocks, w_own, w_mirror, rank):
    m = len(cot_blocks)
    rows, width = cot_blocks[0].shape
    cols = w_own.shape[0]

    def body(rank_ref, *refs):
        cots, w0_ref, w1_ref, g0_ref, g1_ref = refs[:m], *refs[m:]
        for w_ref, g_ref in ((w1_ref, g1_ref), (w0_ref, g0_ref)):
            for j in range(m):
                start = pl.multiple_of((rank_ref[0] ^ j) * rows, rows)
                g_ref[pl.ds(start, rows), :] = dot_nt(cots[j][...], w_ref[...]).astype(BF16)

    full = lambda shape: pl.BlockSpec(shape, lambda i, r: (0, 0))
    return pl.pallas_call(
        body,
        out_shape=[jax.ShapeDtypeStruct((m * rows, cols), BF16)] * 2,
        grid_spec=pltpu.PrefetchScalarGridSpec(
            num_scalar_prefetch=1,
            grid=(1,),
            in_specs=[full((rows, width))] * m + [full((cols, width))] * 2,
            out_specs=[full((m * rows, cols))] * 2,
        ),
        compiler_params=params(),
        cost_estimate=cost(4 * m * rows * width * cols, 2 * width * (m * rows + 2 * cols)),
        name="attention_grad",
    )(rank, *cot_blocks, w_own, w_mirror)


def output_partial(attn_own, attn_mirror, w_own, w_mirror, rank, m):
    tokens, cols = attn_own.shape
    width = w_own.shape[1]
    rows = tokens // m
    step = 512

    def body(rank_ref, a0_ref, a1_ref, w0_ref, w1_ref, *o_refs):
        for j in range(m):
            at = pl.ds(pl.multiple_of((rank_ref[0] ^ j) * rows, rows), rows)
            total = dot_nn(a0_ref[at, :], w0_ref[...]) + dot_nn(a1_ref[at, :], w1_ref[...])
            o_refs[j][...] = total.astype(BF16)

    return pl.pallas_call(
        body,
        out_shape=[jax.ShapeDtypeStruct((rows, width), BF16)] * m,
        grid_spec=pltpu.PrefetchScalarGridSpec(
            num_scalar_prefetch=1,
            grid=(width // step,),
            in_specs=[pl.BlockSpec((tokens, cols), lambda i, r: (0, 0))] * 2
            + [pl.BlockSpec((cols, step), lambda i, r: (0, i))] * 2,
            out_specs=[pl.BlockSpec((rows, step), lambda i, r: (0, i))] * m,
        ),
        compiler_params=params(),
        cost_estimate=cost(4 * tokens * cols * width, 2 * (2 * cols + tokens) * width),
        name="output_partial",
    )(rank, attn_own, attn_mirror, w_own, w_mirror)


def weight_grad_partial(attn_own, attn_mirror, cot_blocks, rank, place, parts):
    m = len(cot_blocks)
    rows, width = cot_blocks[0].shape
    tokens, cols = attn_own.shape
    step = 512
    piece = cols // parts

    def body(rank_ref, place_ref, *refs):
        a0_ref, a1_ref, cots = refs[0], refs[1], refs[2 : 2 + m]
        keep_ref, send_ref, at_ref, sum_ref = refs[2 + m :]

        @pl.when(pl.program_id(0) == 0)
        def _():
            for j in range(m):
                start = pl.multiple_of((rank_ref[0] ^ j) * rows, rows)
                at_ref[j, :cols] = a0_ref[pl.ds(start, rows), :].T
                at_ref[j, cols:] = a1_ref[pl.ds(start, rows), :].T

        total = dot_nn(at_ref[0], cots[0][...])
        for j in range(1, m):
            total += dot_nn(at_ref[j], cots[j][...])
        sum_ref[...] = total.astype(BF16).reshape(2 * parts, piece, step)
        for j in range(parts):
            out_ref = send_ref if j % 2 else keep_ref
            out_ref[j // 2, 0] = sum_ref[place_ref[0] ^ j]
            out_ref[j // 2, 1] = sum_ref[parts + (place_ref[0] ^ j)]

    shape = (parts // 2, 2, piece, width)
    return pl.pallas_call(
        body,
        out_shape=[jax.ShapeDtypeStruct(shape, BF16)] * 2,
        grid_spec=pltpu.PrefetchScalarGridSpec(
            num_scalar_prefetch=2,
            grid=(width // step,),
            in_specs=[pl.BlockSpec((tokens, cols), lambda i, r, p: (0, 0))] * 2
            + [pl.BlockSpec((rows, step), lambda i, r, p: (0, i))] * m,
            out_specs=[pl.BlockSpec(shape[:3] + (step,), lambda i, r, p: (0, 0, 0, i))] * 2,
            scratch_shapes=[
                pltpu.VMEM((m, 2 * cols, rows), BF16),
                pltpu.VMEM((2 * parts, piece, step), BF16),
            ],
        ),
        compiler_params=params(),
        cost_estimate=cost(4 * tokens * cols * width, 2 * (2 * cols + tokens) * width),
        name="weight_grad_partial",
    )(rank, place, attn_own, attn_mirror, *cot_blocks)


def join_parts(pieces, place, dtype):
    parts = len(pieces)
    rows, width = pieces[0].shape
    step = 1024

    def body(place_ref, *refs):
        for j in range(parts):
            refs[parts][place_ref[0] ^ j] = refs[j][...].astype(dtype)

    joined = pl.pallas_call(
        body,
        out_shape=jax.ShapeDtypeStruct((parts, rows, width), dtype),
        grid_spec=pltpu.PrefetchScalarGridSpec(
            num_scalar_prefetch=1,
            grid=(width // step,),
            in_specs=[pl.BlockSpec((rows, step), lambda i, p: (0, i))] * parts,
            out_specs=pl.BlockSpec((parts, rows, step), lambda i, p: (0, 0, i)),
        ),
        compiler_params=params(),
        cost_estimate=cost(0, 6 * parts * rows * width),
        name="join_parts",
    )(place, *pieces)
    return joined.reshape(parts * rows, width)


def key_mask(my_tiles, my_counts, tokens):
    heads, blocks, slots = my_tiles.shape
    key_tile = lax.broadcasted_iota(jnp.int32, (1, blocks, 1, 1), 1)
    slot = lax.broadcasted_iota(jnp.int32, (1, 1, 1, slots), 3)
    seen = (my_tiles[:, None] == key_tile) & (slot < my_counts[:, None, :, None])
    mask = jnp.where(jnp.any(seen, axis=3), F32(0), F32(NEG))
    mask = jnp.pad(mask, ((0, 0), (0, 0), (0, HDIM - blocks)))
    lane = lax.broadcasted_iota(jnp.int32, mask.shape, 2)
    mask = jnp.where(lane >= EXTRA, F32(-1), mask).astype(BF16)
    return jnp.broadcast_to(mask[:, :, None], (heads, blocks, TILE, HDIM)).reshape(
        heads, tokens, HDIM
    )


def shards(queries, key_rows, value_rows, out_weight, cotangent, tile_lists, live_counts):
    n = lax.axis_size("seq")
    dp = lax.axis_size("dp")
    m = n // 2
    s = lax.axis_index("seq")
    d = lax.axis_index("dp")
    half = (s // m).astype(jnp.int32).reshape(1)
    rank = (s % m).astype(jnp.int32).reshape(1)
    rows = queries.shape[1]
    cols, width = out_weight.shape
    heads = cols // HDIM
    place = d.astype(jnp.int32).reshape(1)
    xor = lambda x, bit: lax.ppermute(x, "seq", [(i, i ^ bit) for i in range(n)])

    def gather_parts(x):
        pieces = {0: x}
        bit = dp // 2
        while bit:
            pieces.update({j | bit: dp_xor(x, bit) for j, x in list(pieces.items())})
            bit //= 2
        return [pieces[j] for j in range(dp)]

    dp_xor = lambda x, bit: lax.ppermute(x, "dp", [(i, i ^ bit) for i in range(dp)])

    my_tiles = lax.dynamic_slice_in_dim(tile_lists, s * heads, heads, 0)
    my_counts = lax.dynamic_slice_in_dim(live_counts, s * heads, heads, 0)
    mask = key_mask(my_tiles, my_counts, n * rows)

    packed = pack_heads([queries[0], key_rows[0], value_rows[0]], n)
    packed = lax.all_to_all(packed, "seq", split_axis=0, concat_axis=0, tiled=True)

    attn_own, attn_sent, extra = attention_forward(packed, mask, half)

    piece = cols // dp
    w_piece = xor(lax.dynamic_slice_in_dim(out_weight, d * piece, piece, 0), m)
    bit = m // 2
    cot_at = {0: cotangent[0], bit: xor(cotangent[0], bit)}
    if bit > 1:
        cot_at[1] = xor(cotangent[0], 1)
    attn_send, w_piece, cot_at[bit] = lax.optimization_barrier(
        (attn_sent, w_piece, cot_at[bit])
    )
    attn_mirror = xor(attn_send, m)

    w_pieces = [w_piece] + [dp_xor(w_piece, j) for j in range(1, dp)]
    w_pieces, attn_mirror = lax.optimization_barrier((w_pieces, attn_mirror))
    w_mirror = join_parts(w_pieces, place, BF16)

    while bit > 1:
        bit //= 2
        for j in list(cot_at):
            if j | bit not in cot_at:
                cot_at[j | bit] = xor(cot_at[j], bit)
    cot_blocks = [cot_at[j] for j in range(m)]

    partials = output_partial(attn_own, attn_mirror, out_weight, w_mirror, rank, m)
    partials, cot_blocks = lax.optimization_barrier((partials, cot_blocks))
    partials = dict(enumerate(partials))

    def halve(bit):
        for j in [j for j in sorted(partials, reverse=True) if j & bit and j > bit]:
            got = xor(partials.pop(j), bit).astype(F32)
            partials[j ^ bit] = (partials[j ^ bit].astype(F32) + got).astype(BF16)

    halve(1)
    grad_own, grad_send = attention_grad(cot_blocks, out_weight, w_mirror, rank)
    grad_mirror = xor(grad_send, m)
    attn_mirror, grad_send = lax.optimization_barrier((attn_mirror, grad_send))
    keep, send = weight_grad_partial(attn_own, attn_mirror, cot_blocks, rank, place, dp)
    grad_mirror, keep, send, partials = lax.optimization_barrier(
        (grad_mirror, keep, send, partials)
    )

    gw = keep.astype(F32) + dp_xor(send, 1).astype(F32)
    bit = 2
    while bit < dp:
        gw = gw[0::2].astype(F32) + dp_xor(gw[1::2].astype(BF16), bit).astype(F32)
        bit *= 2
    gw_own, gw_send = gw[0, 0], gw[0, 1].astype(BF16)

    bit = 2
    while bit < m:
        halve(bit)
        bit *= 2
    got = [xor(partials[j], j) for j in sorted(partials) if j]
    grads = []
    for head in range(heads):
        if head == 1:
            gw_send, grad_own = lax.optimization_barrier((gw_send, grad_own))
        grads.append(
            attention_backward(
                packed, mask, half, extra, attn_own, attn_sent, grad_own, grad_mirror, head
            )
        )
    grads[0], got = lax.optimization_barrier((grads[0], got))
    gw = (gw_own + xor(gw_send, m).astype(F32)).astype(BF16)
    grads = [lax.all_to_all(x, "seq", split_axis=0, concat_axis=0, tiled=True) for x in grads]
    back_q, back_k, back_v = unpack_heads(grads)

    block_out = sum(x.astype(F32) for x in [partials[0]] + got).astype(BF16)
    pieces = gather_parts(gw)
    grad_weight = join_parts(pieces, place, F32)
    return (block_out[None], back_q[None], back_k[None], back_v[None], grad_weight)


def solution(mesh):
    token_spec = P("dp", "seq", None)
    in_specs = (
        token_spec,
        token_spec,
        token_spec,
        P("seq", None),
        token_spec,
        P(),
        P(),
    )
    out_specs = (token_spec,) * 4 + (P("seq", None),)
    return jax.shard_map(shards, mesh=mesh, in_specs=in_specs, out_specs=out_specs, check_vma=False)
```

```python
import jax
import jax.numpy as jnp
from jax import lax
from jax.experimental import pallas as pl
from jax.experimental.pallas import tpu as pltpu
from jax.sharding import PartitionSpec as P

HDIM = 128
TILE = 64
SCALE = HDIM**-0.5
EXP2_SCALE = SCALE * 1.4426950408889634
NEG = -1e30
EXTRA = HDIM - 3
VMEM_LIMIT = 48 * 1024 * 1024
BF16 = jnp.bfloat16
F32 = jnp.float32


def params(**kw):
    return pltpu.CompilerParams(vmem_limit_bytes=VMEM_LIMIT, **kw)


def cost(flops, nbytes, exps=0):
    return pl.CostEstimate(flops=flops, bytes_accessed=nbytes, transcendentals=exps)


def dot_nt(a, b):
    return lax.dot_general(a, b, (((1,), (1,)), ((), ())), preferred_element_type=F32)


def dot_nn(a, b):
    return lax.dot_general(a, b, (((1,), (0,)), ((), ())), preferred_element_type=F32)


def pack_heads(arrays, n):
    rows, width = arrays[0].shape
    cols = width // n
    count = len(arrays)

    def body(*refs):
        for a in range(count):
            refs[count][0, a] = refs[a][...]

    return pl.pallas_call(
        body,
        out_shape=jax.ShapeDtypeStruct((n, count, rows, cols), arrays[0].dtype),
        grid=(n,),
        in_specs=[pl.BlockSpec((rows, cols), lambda j: (0, j))] * count,
        out_specs=pl.BlockSpec((1, count, rows, cols), lambda j: (j, 0, 0, 0)),
        compiler_params=params(),
        cost_estimate=cost(0, 4 * n * count * rows * cols),
        name="pack_heads",
    )(*arrays)


def unpack_heads(packed):
    heads = len(packed)
    n, count, rows, width = packed[0].shape
    cols = heads * width

    def body(*refs):
        for a in range(count):
            for h in range(heads):
                refs[heads + a][:, h * width : (h + 1) * width] = refs[h][0, a]

    return pl.pallas_call(
        body,
        out_shape=[jax.ShapeDtypeStruct((rows, n * cols), BF16)] * count,
        grid=(n,),
        in_specs=[pl.BlockSpec((1, count, rows, width), lambda j: (j, 0, 0, 0))] * heads,
        out_specs=[pl.BlockSpec((rows, cols), lambda j: (0, j))] * count,
        compiler_params=params(),
        cost_estimate=cost(0, 4 * n * count * rows * cols),
        name="unpack_heads",
    )(*packed)


def split3(x):
    high = x.astype(BF16)
    rest = x - high.astype(F32)
    mid = rest.astype(BF16)
    low = (rest - mid.astype(F32)).astype(BF16)
    return high, mid, low


def put_columns(base, columns):
    lane = lax.broadcasted_iota(jnp.int32, base.shape, 1)
    for at, column in enumerate(columns):
        base = jnp.where(lane == EXTRA + at, column.astype(F32), base)
    return base


def attention_forward(packed, mask, half):
    n, _, rows, cols = packed.shape
    heads = cols // HDIM
    tokens = n * rows
    q_rows = 2 * rows
    steps = n // 2
    half_steps = steps // 2
    tiles = q_rows // TILE

    def body(half_ref, q_ref, k_ref, v_ref, mask_ref, own_ref, send_ref, extra_ref, wide_ref):
        i = pl.program_id(1)

        @pl.when(i == 0)
        def _():
            wide_ref[:, :HDIM] = k_ref[...].reshape(tokens, HDIM)
            wide_ref[:, HDIM:] = mask_ref[0]

        shape = (q_rows, HDIM)
        tile = lax.broadcasted_iota(jnp.int32, shape, 0) // TILE + i * tiles
        ones = jnp.where(tile == lax.broadcasted_iota(jnp.int32, shape, 1), F32(1), F32(0))
        q = jnp.concatenate([q_ref[...].reshape(shape), ones.astype(BF16)], axis=1)
        v = v_ref[...].reshape(tokens, HDIM)
        sub = q_rows // 2
        starts = range(0, q_rows, sub)
        scores = [dot_nt(q[at : at + sub], wide_ref[...]) for at in starts]
        tops = [jnp.max(s, axis=1, keepdims=True) for s in scores]
        exps = [jnp.exp2((s - top) * EXP2_SCALE) for s, top in zip(scores, tops)]
        totals = [jnp.sum(e, axis=1, keepdims=True) for e in exps]
        attn = [dot_nn(e.astype(BF16), v) * (1.0 / t) for e, t in zip(exps, totals)]
        attn = jnp.concatenate(attn, axis=0).astype(BF16)
        top = jnp.concatenate(tops, axis=0)
        total = jnp.concatenate(totals, axis=0)
        log_sum = top + jnp.log2(total) * (1.0 / EXP2_SCALE)
        extra_ref[...] = put_columns(ones, split3(log_sum)).astype(BF16)
        own = (i // half_steps) == half_ref[0]

        @pl.when(own)
        def _():
            own_ref[...] = attn

        @pl.when(jnp.logical_not(own))
        def _():
            send_ref[...] = attn

    return pl.pallas_call(
        body,
        out_shape=[jax.ShapeDtypeStruct((tokens // 2, cols), BF16)] * 2
        + [jax.ShapeDtypeStruct((tokens, cols), BF16)],
        grid_spec=pltpu.PrefetchScalarGridSpec(
            num_scalar_prefetch=1,
            grid=(heads, steps),
            in_specs=[
                pl.BlockSpec((2, 1, rows, HDIM), lambda h, i, r: (i, 0, 0, h)),
                pl.BlockSpec((n, 1, rows, HDIM), lambda h, i, r: (0, 1, 0, h)),
                pl.BlockSpec((n, 1, rows, HDIM), lambda h, i, r: (0, 2, 0, h)),
                pl.BlockSpec((1, tokens, HDIM), lambda h, i, r: (h, 0, 0)),
            ],
            out_specs=[
                pl.BlockSpec(
                    (q_rows, HDIM),
                    lambda h, i, r: (jnp.clip(i - r[0] * half_steps, 0, half_steps - 1), h),
                ),
                pl.BlockSpec(
                    (q_rows, HDIM),
                    lambda h, i, r: (jnp.clip(i - (1 - r[0]) * half_steps, 0, half_steps - 1), h),
                ),
                pl.BlockSpec((q_rows, HDIM), lambda h, i, r: (i, h)),
            ],
            scratch_shapes=[pltpu.VMEM((tokens, 2 * HDIM), BF16)],
        ),
        compiler_params=params(),
        cost_estimate=cost(4 * tokens**2 * cols, 8 * tokens * cols, heads * tokens**2),
        name="attention_forward",
    )(half, packed, packed, packed, mask)


def attention_backward(packed, mask, half, extra, attn_own, attn_send, grad_own, grad_mirror, head):
    n, _, rows, cols = packed.shape
    tokens = n * rows
    q_rows = 4 * rows
    steps = n // 4
    half_steps = steps // 2

    def body(half_ref, q_ref, k_ref, v_ref, mask_ref, extra_ref, *refs):
        a0_ref, a1_ref, g0_ref, g1_ref, out_ref, dk_ref, dv_ref, wide_ref, wide_v_ref = refs
        i = pl.program_id(0)

        @pl.when(i == 0)
        def _():
            wide_ref[:, :HDIM] = k_ref[...].reshape(tokens, HDIM)
            wide_ref[:, HDIM:] = mask_ref[0]
            wide_v_ref[:, :HDIM] = v_ref[...].reshape(tokens, HDIM)
            lane = lax.broadcasted_iota(jnp.int32, (tokens, HDIM), 1)
            wide_v_ref[:, HDIM:] = jnp.where(lane >= EXTRA, F32(-1), F32(0)).astype(BF16)

        q = q_ref[...].reshape(q_rows, HDIM)
        own = (i // half_steps) == half_ref[0]
        grad = jnp.where(own, g0_ref[...], g1_ref[...])
        attn = jnp.where(own, a0_ref[...], a1_ref[...])
        row_dot = jnp.sum(grad.astype(F32) * attn.astype(F32), axis=1, keepdims=True)
        zeros = jnp.zeros((q_rows, HDIM), F32)
        wide_grad = jnp.concatenate(
            [grad, put_columns(zeros, split3(row_dot)).astype(BF16)], axis=1
        )
        wide_q = jnp.concatenate([q, extra_ref[...]], axis=1)
        probs = jnp.exp2(dot_nt(wide_q, wide_ref[...]) * EXP2_SCALE)
        grad_scores = (probs * dot_nt(wide_grad, wide_v_ref[...])).astype(BF16)
        grad_q = dot_nn(grad_scores, wide_ref[:, :HDIM]) * SCALE
        out_ref[pl.ds(4 * i, 4), 0] = grad_q.astype(BF16).reshape(4, rows, HDIM)
        dk_t = dot_nn(q.T, grad_scores)
        dv_t = dot_nn(grad.T, probs.astype(BF16))

        @pl.when(i == 0)
        def _():
            dk_ref[...] = dk_t
            dv_ref[...] = dv_t

        @pl.when(i > 0)
        def _():
            dk_ref[...] += dk_t
            dv_ref[...] += dv_t

        @pl.when(i == steps - 1)
        def _():
            out_ref[:, 1] = (dk_ref[...] * SCALE).T.astype(BF16).reshape(n, rows, HDIM)
            out_ref[:, 2] = dv_ref[...].T.astype(BF16).reshape(n, rows, HDIM)

    return pl.pallas_call(
        body,
        out_shape=jax.ShapeDtypeStruct((n, 3, rows, HDIM), BF16),
        grid_spec=pltpu.PrefetchScalarGridSpec(
            num_scalar_prefetch=1,
            grid=(steps,),
            in_specs=[
                pl.BlockSpec((4, 1, rows, HDIM), lambda i, r: (i, 0, 0, head)),
                pl.BlockSpec((n, 1, rows, HDIM), lambda i, r: (0, 1, 0, head)),
                pl.BlockSpec((n, 1, rows, HDIM), lambda i, r: (0, 2, 0, head)),
                pl.BlockSpec((1, tokens, HDIM), lambda i, r: (head, 0, 0)),
                pl.BlockSpec((q_rows, HDIM), lambda i, r: (i, head)),
            ]
            + [pl.BlockSpec((q_rows, HDIM), lambda i, r: (i % half_steps, head))] * 4,
            out_specs=pl.BlockSpec((n, 3, rows, HDIM), lambda i, r: (0, 0, 0, 0)),
            scratch_shapes=[pltpu.VMEM((HDIM, tokens), F32)] * 2
            + [pltpu.VMEM((tokens, 2 * HDIM), BF16)] * 2,
        ),
        compiler_params=params(),
        cost_estimate=cost(10 * tokens**2 * HDIM, 14 * tokens * HDIM, tokens**2),
        name="attention_backward",
    )(half, packed, packed, packed, mask, extra, attn_own, attn_send, grad_own, grad_mirror)


def attention_grad(cot_blocks, w_own, w_mirror, rank):
    m = len(cot_blocks)
    rows, width = cot_blocks[0].shape
    cols = w_own.shape[0]

    def body(rank_ref, *refs):
        cots, w0_ref, w1_ref, g0_ref, g1_ref = refs[:m], *refs[m:]
        for w_ref, g_ref in ((w1_ref, g1_ref), (w0_ref, g0_ref)):
            for j in range(m):
                start = pl.multiple_of((rank_ref[0] ^ j) * rows, rows)
                g_ref[pl.ds(start, rows), :] = dot_nt(cots[j][...], w_ref[...]).astype(BF16)

    full = lambda shape: pl.BlockSpec(shape, lambda i, r: (0, 0))
    return pl.pallas_call(
        body,
        out_shape=[jax.ShapeDtypeStruct((m * rows, cols), BF16)] * 2,
        grid_spec=pltpu.PrefetchScalarGridSpec(
            num_scalar_prefetch=1,
            grid=(1,),
            in_specs=[full((rows, width))] * m + [full((cols, width))] * 2,
            out_specs=[full((m * rows, cols))] * 2,
        ),
        compiler_params=params(),
        cost_estimate=cost(4 * m * rows * width * cols, 2 * width * (m * rows + 2 * cols)),
        name="attention_grad",
    )(rank, *cot_blocks, w_own, w_mirror)


def output_partial(attn_own, attn_mirror, w_own, w_mirror, rank, m):
    tokens, cols = attn_own.shape
    width = w_own.shape[1]
    rows = tokens // m
    step = 512

    def body(rank_ref, a0_ref, a1_ref, w0_ref, w1_ref, *o_refs):
        for j in range(m):
            at = pl.ds(pl.multiple_of((rank_ref[0] ^ j) * rows, rows), rows)
            total = dot_nn(a0_ref[at, :], w0_ref[...]) + dot_nn(a1_ref[at, :], w1_ref[...])
            o_refs[j][...] = total.astype(BF16)

    return pl.pallas_call(
        body,
        out_shape=[jax.ShapeDtypeStruct((rows, width), BF16)] * m,
        grid_spec=pltpu.PrefetchScalarGridSpec(
            num_scalar_prefetch=1,
            grid=(width // step,),
            in_specs=[pl.BlockSpec((tokens, cols), lambda i, r: (0, 0))] * 2
            + [pl.BlockSpec((cols, step), lambda i, r: (0, i))] * 2,
            out_specs=[pl.BlockSpec((rows, step), lambda i, r: (0, i))] * m,
        ),
        compiler_params=params(),
        cost_estimate=cost(4 * tokens * cols * width, 2 * (2 * cols + tokens) * width),
        name="output_partial",
    )(rank, attn_own, attn_mirror, w_own, w_mirror)


def weight_grad_partial(attn_own, attn_mirror, cot_blocks, rank, place, parts):
    m = len(cot_blocks)
    rows, width = cot_blocks[0].shape
    tokens, cols = attn_own.shape
    step = 512
    piece = cols // parts

    def body(rank_ref, place_ref, *refs):
        a0_ref, a1_ref, cots = refs[0], refs[1], refs[2 : 2 + m]
        keep_ref, send_ref, at_ref, sum_ref = refs[2 + m :]

        @pl.when(pl.program_id(0) == 0)
        def _():
            for j in range(m):
                at = pl.ds(pl.multiple_of((rank_ref[0] ^ j) * rows, rows), rows)
                at_ref[:cols, j * rows : (j + 1) * rows] = a0_ref[at, :].T
                at_ref[cols:, j * rows : (j + 1) * rows] = a1_ref[at, :].T

        total = dot_nn(at_ref[...], jnp.concatenate([c[...] for c in cots], axis=0))
        sum_ref[...] = total.astype(BF16).reshape(2 * parts, piece, step)
        for j in range(parts):
            out_ref = send_ref if j % 2 else keep_ref
            out_ref[j // 2, 0] = sum_ref[place_ref[0] ^ j]
            out_ref[j // 2, 1] = sum_ref[parts + (place_ref[0] ^ j)]

    shape = (parts // 2, 2, piece, width)
    return pl.pallas_call(
        body,
        out_shape=[jax.ShapeDtypeStruct(shape, BF16)] * 2,
        grid_spec=pltpu.PrefetchScalarGridSpec(
            num_scalar_prefetch=2,
            grid=(width // step,),
            in_specs=[pl.BlockSpec((tokens, cols), lambda i, r, p: (0, 0))] * 2
            + [pl.BlockSpec((rows, step), lambda i, r, p: (0, i))] * m,
            out_specs=[pl.BlockSpec(shape[:3] + (step,), lambda i, r, p: (0, 0, 0, i))] * 2,
            scratch_shapes=[
                pltpu.VMEM((2 * cols, m * rows), BF16),
                pltpu.VMEM((2 * parts, piece, step), BF16),
            ],
        ),
        compiler_params=params(),
        cost_estimate=cost(4 * tokens * cols * width, 2 * (2 * cols + tokens) * width),
        name="weight_grad_partial",
    )(rank, place, attn_own, attn_mirror, *cot_blocks)


def join_parts(pieces, place, dtype):
    parts = len(pieces)
    rows, width = pieces[0].shape
    step = 1024

    def body(place_ref, *refs):
        for j in range(parts):
            refs[parts][place_ref[0] ^ j] = refs[j][...].astype(dtype)

    joined = pl.pallas_call(
        body,
        out_shape=jax.ShapeDtypeStruct((parts, rows, width), dtype),
        grid_spec=pltpu.PrefetchScalarGridSpec(
            num_scalar_prefetch=1,
            grid=(width // step,),
            in_specs=[pl.BlockSpec((rows, step), lambda i, p: (0, i))] * parts,
            out_specs=pl.BlockSpec((parts, rows, step), lambda i, p: (0, 0, i)),
        ),
        compiler_params=params(),
        cost_estimate=cost(0, 6 * parts * rows * width),
        name="join_parts",
    )(place, *pieces)
    return joined.reshape(parts * rows, width)


def key_mask(my_tiles, my_counts, tokens):
    heads, blocks, slots = my_tiles.shape
    key_tile = lax.broadcasted_iota(jnp.int32, (1, blocks, 1, 1), 1)
    slot = lax.broadcasted_iota(jnp.int32, (1, 1, 1, slots), 3)
    seen = (my_tiles[:, None] == key_tile) & (slot < my_counts[:, None, :, None])
    mask = jnp.where(jnp.any(seen, axis=3), F32(0), F32(NEG))
    mask = jnp.pad(mask, ((0, 0), (0, 0), (0, HDIM - blocks)))
    lane = lax.broadcasted_iota(jnp.int32, mask.shape, 2)
    mask = jnp.where(lane >= EXTRA, F32(-1), mask).astype(BF16)
    return jnp.broadcast_to(mask[:, :, None], (heads, blocks, TILE, HDIM)).reshape(
        heads, tokens, HDIM
    )


def shards(queries, key_rows, value_rows, out_weight, cotangent, tile_lists, live_counts):
    n = lax.axis_size("seq")
    dp = lax.axis_size("dp")
    m = n // 2
    s = lax.axis_index("seq")
    d = lax.axis_index("dp")
    half = (s // m).astype(jnp.int32).reshape(1)
    rank = (s % m).astype(jnp.int32).reshape(1)
    rows = queries.shape[1]
    cols, width = out_weight.shape
    heads = cols // HDIM
    place = d.astype(jnp.int32).reshape(1)
    xor = lambda x, bit: lax.ppermute(x, "seq", [(i, i ^ bit) for i in range(n)])

    def gather_parts(x):
        pieces = {0: x}
        bit = dp // 2
        while bit:
            pieces.update({j | bit: dp_xor(x, bit) for j, x in list(pieces.items())})
            bit //= 2
        return [pieces[j] for j in range(dp)]

    dp_xor = lambda x, bit: lax.ppermute(x, "dp", [(i, i ^ bit) for i in range(dp)])

    my_tiles = lax.dynamic_slice_in_dim(tile_lists, s * heads, heads, 0)
    my_counts = lax.dynamic_slice_in_dim(live_counts, s * heads, heads, 0)
    mask = key_mask(my_tiles, my_counts, n * rows)

    packed = pack_heads([queries[0], key_rows[0], value_rows[0]], n)
    packed = lax.all_to_all(packed, "seq", split_axis=0, concat_axis=0, tiled=True)

    attn_own, attn_sent, extra = attention_forward(packed, mask, half)

    piece = cols // dp
    w_piece = xor(lax.dynamic_slice_in_dim(out_weight, d * piece, piece, 0), m)
    bit = m // 2
    cot_at = {0: cotangent[0], bit: xor(cotangent[0], bit)}
    if bit > 1:
        cot_at[1] = xor(cotangent[0], 1)
    attn_send, w_piece, cot_at[bit] = lax.optimization_barrier(
        (attn_sent, w_piece, cot_at[bit])
    )
    attn_mirror = xor(attn_send, m)

    w_pieces = [w_piece] + [dp_xor(w_piece, j) for j in range(1, dp)]
    w_pieces, attn_mirror = lax.optimization_barrier((w_pieces, attn_mirror))
    w_mirror = join_parts(w_pieces, place, BF16)

    while bit > 1:
        bit //= 2
        for j in list(cot_at):
            if j | bit not in cot_at:
                cot_at[j | bit] = xor(cot_at[j], bit)
    cot_blocks = [cot_at[j] for j in range(m)]

    partials = output_partial(attn_own, attn_mirror, out_weight, w_mirror, rank, m)
    partials, cot_blocks = lax.optimization_barrier((partials, cot_blocks))
    partials = dict(enumerate(partials))

    def halve(bit):
        for j in [j for j in sorted(partials, reverse=True) if j & bit and j > bit]:
            got = xor(partials.pop(j), bit).astype(F32)
            partials[j ^ bit] = (partials[j ^ bit].astype(F32) + got).astype(BF16)

    halve(1)
    grad_own, grad_send = attention_grad(cot_blocks, out_weight, w_mirror, rank)
    grad_mirror = xor(grad_send, m)
    attn_mirror, grad_send = lax.optimization_barrier((attn_mirror, grad_send))
    keep, send = weight_grad_partial(attn_own, attn_mirror, cot_blocks, rank, place, dp)
    grad_mirror, keep, send, partials = lax.optimization_barrier(
        (grad_mirror, keep, send, partials)
    )

    gw = keep.astype(F32) + dp_xor(send, 1).astype(F32)
    bit = 2
    while bit < dp:
        gw = gw[0::2].astype(F32) + dp_xor(gw[1::2].astype(BF16), bit).astype(F32)
        bit *= 2
    gw_own, gw_send = gw[0, 0], gw[0, 1].astype(BF16)

    bit = 2
    while bit < m:
        halve(bit)
        bit *= 2
    got = [xor(partials[j], j) for j in sorted(partials) if j]
    grads = []
    for head in range(heads):
        if head == 1:
            gw_send, grad_own = lax.optimization_barrier((gw_send, grad_own))
        grads.append(
            attention_backward(
                packed, mask, half, extra, attn_own, attn_sent, grad_own, grad_mirror, head
            )
        )
    grads[0], got = lax.optimization_barrier((grads[0], got))
    gw = (gw_own + xor(gw_send, m).astype(F32)).astype(BF16)
    grads = [lax.all_to_all(x, "seq", split_axis=0, concat_axis=0, tiled=True) for x in grads]
    back_q, back_k, back_v = unpack_heads(grads)

    block_out = sum(x.astype(F32) for x in [partials[0]] + got).astype(BF16)
    pieces = gather_parts(gw)
    grad_weight = join_parts(pieces, place, F32)
    return (block_out[None], back_q[None], back_k[None], back_v[None], grad_weight)


def solution(mesh):
    token_spec = P("dp", "seq", None)
    in_specs = (
        token_spec,
        token_spec,
        token_spec,
        P("seq", None),
        token_spec,
        P(),
        P(),
    )
    out_specs = (token_spec,) * 4 + (P("seq", None),)
    return jax.shard_map(shards, mesh=mesh, in_specs=in_specs, out_specs=out_specs, check_vma=False)
```

```python
import jax
import jax.numpy as jnp
from jax import lax
from jax.experimental import pallas as pl
from jax.experimental.pallas import tpu as pltpu
from jax.sharding import PartitionSpec as P

HDIM = 128
TILE = 64
SCALE = HDIM**-0.5
EXP2_SCALE = SCALE * 1.4426950408889634
NEG = -1e30
EXTRA = HDIM - 3
VMEM_LIMIT = 48 * 1024 * 1024
BF16 = jnp.bfloat16
F32 = jnp.float32


def params(**kw):
    return pltpu.CompilerParams(vmem_limit_bytes=VMEM_LIMIT, **kw)


def cost(flops, nbytes, exps=0):
    return pl.CostEstimate(flops=flops, bytes_accessed=nbytes, transcendentals=exps)


def dot_nt(a, b):
    return lax.dot_general(a, b, (((1,), (1,)), ((), ())), preferred_element_type=F32)


def dot_nn(a, b):
    return lax.dot_general(a, b, (((1,), (0,)), ((), ())), preferred_element_type=F32)


def pack_heads(arrays, n):
    rows, width = arrays[0].shape
    cols = width // n
    count = len(arrays)

    def body(*refs):
        for a in range(count):
            refs[count][0, a] = refs[a][...]

    return pl.pallas_call(
        body,
        out_shape=jax.ShapeDtypeStruct((n, count, rows, cols), arrays[0].dtype),
        grid=(n,),
        in_specs=[pl.BlockSpec((rows, cols), lambda j: (0, j))] * count,
        out_specs=pl.BlockSpec((1, count, rows, cols), lambda j: (j, 0, 0, 0)),
        compiler_params=params(),
        cost_estimate=cost(0, 4 * n * count * rows * cols),
        name="pack_heads",
    )(*arrays)


def unpack_head(packed, head, heads, outs):
    n, count, rows, width = packed.shape

    def body(*refs):
        for a in range(count):
            refs[1 + len(outs) + a][...] = refs[0][0, a]

    return pl.pallas_call(
        body,
        out_shape=[jax.ShapeDtypeStruct((rows, n * heads * width), BF16)] * count,
        grid=(n,),
        in_specs=[pl.BlockSpec((1, count, rows, width), lambda j: (j, 0, 0, 0))]
        + [pl.BlockSpec(memory_space=pl.ANY)] * len(outs),
        out_specs=[pl.BlockSpec((rows, width), lambda j: (0, j * heads + head))] * count,
        input_output_aliases={1 + a: a for a in range(len(outs))},
        compiler_params=params(),
        cost_estimate=cost(0, 4 * n * count * rows * width),
        name="unpack_head",
    )(packed, *outs)


def split3(x):
    high = x.astype(BF16)
    rest = x - high.astype(F32)
    mid = rest.astype(BF16)
    low = (rest - mid.astype(F32)).astype(BF16)
    return high, mid, low


def put_columns(base, columns):
    lane = lax.broadcasted_iota(jnp.int32, base.shape, 1)
    for at, column in enumerate(columns):
        base = jnp.where(lane == EXTRA + at, column.astype(F32), base)
    return base


def attention_forward(packed, mask, half):
    n, _, rows, cols = packed.shape
    heads = cols // HDIM
    tokens = n * rows
    q_rows = 2 * rows
    steps = n // 2
    half_steps = steps // 2
    tiles = q_rows // TILE

    def body(half_ref, q_ref, k_ref, v_ref, mask_ref, own_ref, send_ref, extra_ref, wide_ref):
        i = pl.program_id(1)

        @pl.when(i == 0)
        def _():
            wide_ref[:, :HDIM] = k_ref[...].reshape(tokens, HDIM)
            wide_ref[:, HDIM:] = mask_ref[0]

        shape = (q_rows, HDIM)
        tile = lax.broadcasted_iota(jnp.int32, shape, 0) // TILE + i * tiles
        ones = jnp.where(tile == lax.broadcasted_iota(jnp.int32, shape, 1), F32(1), F32(0))
        q = jnp.concatenate([q_ref[...].reshape(shape), ones.astype(BF16)], axis=1)
        s = dot_nt(q, wide_ref[...])
        top = jnp.max(s, axis=1, keepdims=True)
        e = jnp.exp2((s - top) * EXP2_SCALE)
        total = jnp.sum(e, axis=1, keepdims=True)
        attn = dot_nn(e.astype(BF16), v_ref[...].reshape(tokens, HDIM)) * (1.0 / total)
        attn = attn.astype(BF16)
        log_sum = top + jnp.log2(total) * (1.0 / EXP2_SCALE)
        extra_ref[...] = put_columns(ones, split3(log_sum)).astype(BF16)
        own = (i // half_steps) == half_ref[0]

        @pl.when(own)
        def _():
            own_ref[...] = attn

        @pl.when(jnp.logical_not(own))
        def _():
            send_ref[...] = attn

    return pl.pallas_call(
        body,
        out_shape=[jax.ShapeDtypeStruct((tokens // 2, cols), BF16)] * 2
        + [jax.ShapeDtypeStruct((tokens, cols), BF16)],
        grid_spec=pltpu.PrefetchScalarGridSpec(
            num_scalar_prefetch=1,
            grid=(heads, steps),
            in_specs=[
                pl.BlockSpec((2, 1, rows, HDIM), lambda h, i, r: (i, 0, 0, h)),
                pl.BlockSpec((n, 1, rows, HDIM), lambda h, i, r: (0, 1, 0, h)),
                pl.BlockSpec((n, 1, rows, HDIM), lambda h, i, r: (0, 2, 0, h)),
                pl.BlockSpec((1, tokens, HDIM), lambda h, i, r: (h, 0, 0)),
            ],
            out_specs=[
                pl.BlockSpec(
                    (q_rows, HDIM),
                    lambda h, i, r: (jnp.clip(i - r[0] * half_steps, 0, half_steps - 1), h),
                ),
                pl.BlockSpec(
                    (q_rows, HDIM),
                    lambda h, i, r: (jnp.clip(i - (1 - r[0]) * half_steps, 0, half_steps - 1), h),
                ),
                pl.BlockSpec((q_rows, HDIM), lambda h, i, r: (i, h)),
            ],
            scratch_shapes=[pltpu.VMEM((tokens, 2 * HDIM), BF16)],
        ),
        compiler_params=params(),
        cost_estimate=cost(4 * tokens**2 * cols, 8 * tokens * cols, heads * tokens**2),
        name="attention_forward",
    )(half, packed, packed, packed, mask)


def attention_backward(packed, mask, half, extra, attn_own, attn_send, grad_own, grad_mirror, head):
    n, _, rows, cols = packed.shape
    tokens = n * rows
    q_rows = 2 * rows
    steps = n // 2
    half_steps = steps // 2

    def body(half_ref, q_ref, k_ref, v_ref, mask_ref, extra_ref, *refs):
        a0_ref, a1_ref, g0_ref, g1_ref, out_ref, dk_ref, dv_ref, wide_ref, wide_v_ref = refs
        i = pl.program_id(0)

        @pl.when(i == 0)
        def _():
            wide_ref[:, :HDIM] = k_ref[...].reshape(tokens, HDIM)
            wide_ref[:, HDIM:] = mask_ref[0]
            wide_v_ref[:, :HDIM] = v_ref[...].reshape(tokens, HDIM)
            lane = lax.broadcasted_iota(jnp.int32, (tokens, HDIM), 1)
            wide_v_ref[:, HDIM:] = jnp.where(lane >= EXTRA, F32(-1), F32(0)).astype(BF16)

        q = q_ref[...].reshape(q_rows, HDIM)
        own = (i // half_steps) == half_ref[0]
        grad = jnp.where(own, g0_ref[...], g1_ref[...])
        attn = jnp.where(own, a0_ref[...], a1_ref[...])
        row_dot = jnp.sum(grad.astype(F32) * attn.astype(F32), axis=1, keepdims=True)
        zeros = jnp.zeros((q_rows, HDIM), F32)
        wide_grad = jnp.concatenate(
            [grad, put_columns(zeros, split3(row_dot)).astype(BF16)], axis=1
        )
        wide_q = jnp.concatenate([q, extra_ref[...]], axis=1)
        probs = jnp.exp2(dot_nt(wide_q, wide_ref[...]) * EXP2_SCALE)
        grad_scores = (probs * dot_nt(wide_grad, wide_v_ref[...])).astype(BF16)
        grad_q = dot_nn(grad_scores, wide_ref[:, :HDIM]) * SCALE
        out_ref[pl.ds(2 * i, 2), 0] = grad_q.astype(BF16).reshape(2, rows, HDIM)
        dk_t = dot_nn(q.T, grad_scores)
        dv_t = dot_nn(grad.T, probs.astype(BF16))

        @pl.when(i == 0)
        def _():
            dk_ref[...] = dk_t
            dv_ref[...] = dv_t

        @pl.when(i > 0)
        def _():
            dk_ref[...] += dk_t
            dv_ref[...] += dv_t

        @pl.when(i == steps - 1)
        def _():
            out_ref[:, 1] = (dk_ref[...] * SCALE).T.astype(BF16).reshape(n, rows, HDIM)
            out_ref[:, 2] = dv_ref[...].T.astype(BF16).reshape(n, rows, HDIM)

    return pl.pallas_call(
        body,
        out_shape=jax.ShapeDtypeStruct((n, 3, rows, HDIM), BF16),
        grid_spec=pltpu.PrefetchScalarGridSpec(
            num_scalar_prefetch=1,
            grid=(steps,),
            in_specs=[
                pl.BlockSpec((2, 1, rows, HDIM), lambda i, r: (i, 0, 0, head)),
                pl.BlockSpec((n, 1, rows, HDIM), lambda i, r: (0, 1, 0, head)),
                pl.BlockSpec((n, 1, rows, HDIM), lambda i, r: (0, 2, 0, head)),
                pl.BlockSpec((1, tokens, HDIM), lambda i, r: (head, 0, 0)),
                pl.BlockSpec((q_rows, HDIM), lambda i, r: (i, head)),
            ]
            + [pl.BlockSpec((q_rows, HDIM), lambda i, r: (i % half_steps, head))] * 4,
            out_specs=pl.BlockSpec((n, 3, rows, HDIM), lambda i, r: (0, 0, 0, 0)),
            scratch_shapes=[pltpu.VMEM((HDIM, tokens), F32)] * 2
            + [pltpu.VMEM((tokens, 2 * HDIM), BF16)] * 2,
        ),
        compiler_params=params(),
        cost_estimate=cost(10 * tokens**2 * HDIM, 14 * tokens * HDIM, tokens**2),
        name="attention_backward",
    )(half, packed, packed, packed, mask, extra, attn_own, attn_send, grad_own, grad_mirror)


def attention_grad(cot_blocks, w_own, w_mirror, rank):
    m = len(cot_blocks)
    rows, width = cot_blocks[0].shape
    cols = w_own.shape[0]

    def body(rank_ref, *refs):
        cots, w0_ref, w1_ref, g0_ref, g1_ref = refs[:m], *refs[m:]
        for w_ref, g_ref in ((w1_ref, g1_ref), (w0_ref, g0_ref)):
            for j in range(m):
                start = pl.multiple_of((rank_ref[0] ^ j) * rows, rows)
                g_ref[pl.ds(start, rows), :] = dot_nt(cots[j][...], w_ref[...]).astype(BF16)

    full = lambda shape: pl.BlockSpec(shape, lambda i, r: (0, 0))
    return pl.pallas_call(
        body,
        out_shape=[jax.ShapeDtypeStruct((m * rows, cols), BF16)] * 2,
        grid_spec=pltpu.PrefetchScalarGridSpec(
            num_scalar_prefetch=1,
            grid=(1,),
            in_specs=[full((rows, width))] * m + [full((cols, width))] * 2,
            out_specs=[full((m * rows, cols))] * 2,
        ),
        compiler_params=params(),
        cost_estimate=cost(4 * m * rows * width * cols, 2 * width * (m * rows + 2 * cols)),
        name="attention_grad",
    )(rank, *cot_blocks, w_own, w_mirror)


def output_partial(attn_own, attn_mirror, w_own, w_mirror, rank, m):
    tokens, cols = attn_own.shape
    width = w_own.shape[1]
    rows = tokens // m
    step = 512

    def body(rank_ref, a0_ref, a1_ref, w0_ref, w1_ref, *o_refs):
        for j in range(m):
            at = pl.ds(pl.multiple_of((rank_ref[0] ^ j) * rows, rows), rows)
            total = dot_nn(a0_ref[at, :], w0_ref[...]) + dot_nn(a1_ref[at, :], w1_ref[...])
            o_refs[j][...] = total.astype(BF16)

    return pl.pallas_call(
        body,
        out_shape=[jax.ShapeDtypeStruct((rows, width), BF16)] * m,
        grid_spec=pltpu.PrefetchScalarGridSpec(
            num_scalar_prefetch=1,
            grid=(width // step,),
            in_specs=[pl.BlockSpec((tokens, cols), lambda i, r: (0, 0))] * 2
            + [pl.BlockSpec((cols, step), lambda i, r: (0, i))] * 2,
            out_specs=[pl.BlockSpec((rows, step), lambda i, r: (0, i))] * m,
        ),
        compiler_params=params(),
        cost_estimate=cost(4 * tokens * cols * width, 2 * (2 * cols + tokens) * width),
        name="output_partial",
    )(rank, attn_own, attn_mirror, w_own, w_mirror)


def weight_grad_partial(attn_own, attn_mirror, cot_blocks, rank, place, parts):
    m = len(cot_blocks)
    rows, width = cot_blocks[0].shape
    tokens, cols = attn_own.shape
    step = 512
    piece = cols // parts

    def body(rank_ref, place_ref, *refs):
        a0_ref, a1_ref, cots = refs[0], refs[1], refs[2 : 2 + m]
        keep_ref, send_ref, at_ref, sum_ref = refs[2 + m :]

        @pl.when(pl.program_id(0) == 0)
        def _():
            for j in range(m):
                start = pl.multiple_of((rank_ref[0] ^ j) * rows, rows)
                at_ref[j, :cols] = a0_ref[pl.ds(start, rows), :].T
                at_ref[j, cols:] = a1_ref[pl.ds(start, rows), :].T

        total = dot_nn(at_ref[0], cots[0][...])
        for j in range(1, m):
            total += dot_nn(at_ref[j], cots[j][...])
        sum_ref[...] = total.astype(BF16).reshape(2 * parts, piece, step)
        for j in range(parts):
            out_ref = send_ref if j % 2 else keep_ref
            out_ref[j // 2, 0] = sum_ref[place_ref[0] ^ j]
            out_ref[j // 2, 1] = sum_ref[parts + (place_ref[0] ^ j)]

    shape = (parts // 2, 2, piece, width)
    return pl.pallas_call(
        body,
        out_shape=[jax.ShapeDtypeStruct(shape, BF16)] * 2,
        grid_spec=pltpu.PrefetchScalarGridSpec(
            num_scalar_prefetch=2,
            grid=(width // step,),
            in_specs=[pl.BlockSpec((tokens, cols), lambda i, r, p: (0, 0))] * 2
            + [pl.BlockSpec((rows, step), lambda i, r, p: (0, i))] * m,
            out_specs=[pl.BlockSpec(shape[:3] + (step,), lambda i, r, p: (0, 0, 0, i))] * 2,
            scratch_shapes=[
                pltpu.VMEM((m, 2 * cols, rows), BF16),
                pltpu.VMEM((2 * parts, piece, step), BF16),
            ],
        ),
        compiler_params=params(),
        cost_estimate=cost(4 * tokens * cols * width, 2 * (2 * cols + tokens) * width),
        name="weight_grad_partial",
    )(rank, place, attn_own, attn_mirror, *cot_blocks)


def join_parts(pieces, place, dtype):
    parts = len(pieces)
    rows, width = pieces[0].shape
    step = 1024

    def body(place_ref, *refs):
        for j in range(parts):
            refs[parts][place_ref[0] ^ j] = refs[j][...].astype(dtype)

    joined = pl.pallas_call(
        body,
        out_shape=jax.ShapeDtypeStruct((parts, rows, width), dtype),
        grid_spec=pltpu.PrefetchScalarGridSpec(
            num_scalar_prefetch=1,
            grid=(width // step,),
            in_specs=[pl.BlockSpec((rows, step), lambda i, p: (0, i))] * parts,
            out_specs=pl.BlockSpec((parts, rows, step), lambda i, p: (0, 0, i)),
        ),
        compiler_params=params(),
        cost_estimate=cost(0, 6 * parts * rows * width),
        name="join_parts",
    )(place, *pieces)
    return joined.reshape(parts * rows, width)


def key_mask(my_tiles, my_counts, tokens):
    heads, blocks, slots = my_tiles.shape
    key_tile = lax.broadcasted_iota(jnp.int32, (1, blocks, 1, 1), 1)
    slot = lax.broadcasted_iota(jnp.int32, (1, 1, 1, slots), 3)
    seen = (my_tiles[:, None] == key_tile) & (slot < my_counts[:, None, :, None])
    mask = jnp.where(jnp.any(seen, axis=3), F32(0), F32(NEG))
    mask = jnp.pad(mask, ((0, 0), (0, 0), (0, HDIM - blocks)))
    lane = lax.broadcasted_iota(jnp.int32, mask.shape, 2)
    mask = jnp.where(lane >= EXTRA, F32(-1), mask).astype(BF16)
    return jnp.broadcast_to(mask[:, :, None], (heads, blocks, TILE, HDIM)).reshape(
        heads, tokens, HDIM
    )


def shards(queries, key_rows, value_rows, out_weight, cotangent, tile_lists, live_counts):
    n = lax.axis_size("seq")
    dp = lax.axis_size("dp")
    m = n // 2
    s = lax.axis_index("seq")
    d = lax.axis_index("dp")
    half = (s // m).astype(jnp.int32).reshape(1)
    rank = (s % m).astype(jnp.int32).reshape(1)
    rows = queries.shape[1]
    cols, width = out_weight.shape
    heads = cols // HDIM
    place = d.astype(jnp.int32).reshape(1)
    xor = lambda x, bit: lax.ppermute(x, "seq", [(i, i ^ bit) for i in range(n)])

    def gather_parts(x):
        pieces = {0: x}
        bit = dp // 2
        while bit:
            pieces.update({j | bit: dp_xor(x, bit) for j, x in list(pieces.items())})
            bit //= 2
        return [pieces[j] for j in range(dp)]

    dp_xor = lambda x, bit: lax.ppermute(x, "dp", [(i, i ^ bit) for i in range(dp)])

    my_tiles = lax.dynamic_slice_in_dim(tile_lists, s * heads, heads, 0)
    my_counts = lax.dynamic_slice_in_dim(live_counts, s * heads, heads, 0)
    mask = key_mask(my_tiles, my_counts, n * rows)

    packed = pack_heads([queries[0], key_rows[0], value_rows[0]], n)
    packed = lax.all_to_all(packed, "seq", split_axis=0, concat_axis=0, tiled=True)

    attn_own, attn_sent, extra = attention_forward(packed, mask, half)

    piece = cols // dp
    w_piece = xor(lax.dynamic_slice_in_dim(out_weight, d * piece, piece, 0), m)
    bit = m // 2
    cot_at = {0: cotangent[0], bit: xor(cotangent[0], bit)}
    if bit > 1:
        cot_at[1] = xor(cotangent[0], 1)
    attn_send, w_piece, cot_at[bit] = lax.optimization_barrier(
        (attn_sent, w_piece, cot_at[bit])
    )
    attn_mirror = xor(attn_send, m)

    w_pieces = [w_piece] + [dp_xor(w_piece, j) for j in range(1, dp)]
    w_pieces, attn_mirror = lax.optimization_barrier((w_pieces, attn_mirror))
    w_mirror = join_parts(w_pieces, place, BF16)

    while bit > 1:
        bit //= 2
        for j in list(cot_at):
            if j | bit not in cot_at:
                cot_at[j | bit] = xor(cot_at[j], bit)
    cot_blocks = [cot_at[j] for j in range(m)]

    partials = output_partial(attn_own, attn_mirror, out_weight, w_mirror, rank, m)
    partials, cot_blocks = lax.optimization_barrier((partials, cot_blocks))
    partials = dict(enumerate(partials))

    def halve(bit):
        for j in [j for j in sorted(partials, reverse=True) if j & bit and j > bit]:
            got = xor(partials.pop(j), bit).astype(F32)
            partials[j ^ bit] = (partials[j ^ bit].astype(F32) + got).astype(BF16)

    halve(1)
    grad_own, grad_send = attention_grad(cot_blocks, out_weight, w_mirror, rank)
    grad_mirror = xor(grad_send, m)
    attn_mirror, grad_send = lax.optimization_barrier((attn_mirror, grad_send))
    keep, send = weight_grad_partial(attn_own, attn_mirror, cot_blocks, rank, place, dp)
    grad_mirror, keep, send, partials = lax.optimization_barrier(
        (grad_mirror, keep, send, partials)
    )

    gw = keep.astype(F32) + dp_xor(send, 1).astype(F32)
    bit = 2
    while bit < dp:
        gw = gw[0::2].astype(F32) + dp_xor(gw[1::2].astype(BF16), bit).astype(F32)
        bit *= 2
    gw_own, gw_send = gw[0, 0], gw[0, 1].astype(BF16)

    bit = 2
    while bit < m:
        halve(bit)
        bit *= 2
    got = [xor(partials[j], j) for j in sorted(partials) if j]
    grads = []
    for head in range(heads):
        if head == 1:
            gw_send, grad_own = lax.optimization_barrier((gw_send, grad_own))
        grads.append(
            attention_backward(
                packed, mask, half, extra, attn_own, attn_sent, grad_own, grad_mirror, head
            )
        )
    grads[0], got = lax.optimization_barrier((grads[0], got))
    gw = (gw_own + xor(gw_send, m).astype(F32)).astype(BF16)
    grads = [lax.all_to_all(x, "seq", split_axis=0, concat_axis=0, tiled=True) for x in grads]
    back = []
    for head in range(heads):
        back = unpack_head(grads[head], head, heads, back)
    back_q, back_k, back_v = back

    block_out = sum(x.astype(F32) for x in [partials[0]] + got).astype(BF16)
    pieces = gather_parts(gw)
    grad_weight = join_parts(pieces, place, F32)
    return (block_out[None], back_q[None], back_k[None], back_v[None], grad_weight)


def solution(mesh):
    token_spec = P("dp", "seq", None)
    in_specs = (
        token_spec,
        token_spec,
        token_spec,
        P("seq", None),
        token_spec,
        P(),
        P(),
    )
    out_specs = (token_spec,) * 4 + (P("seq", None),)
    return jax.shard_map(shards, mesh=mesh, in_specs=in_specs, out_specs=out_specs, check_vma=False)
```
